512 devices in a mesh: src: 8 (over z_lo, core), lat: 32 (over y, x), sub: 2 (over z_hi).
Axes of the slice: x: 4, y: 8, z: 8 (z_hi: 2, z_lo: 4; z = z_hi * 4 + z_lo), core: 2. Of those that a mesh axis runs over, the one named last changes fastest.
Arguments:
- sources: float32 [8, 24, 384, 8, 128], P(None, None, ('lat', 'sub'), 'src'), may hold values from -6 to 6
- eigvecs: bfloat16 [32, 24, 384, 8, 128], P(None, None, ('lat', 'sub'), 'src'), may hold values from -6 to 6
- eigvals: float32 [32], replicated, may hold values from 0.5 to 8
- links: float32 [4, 18, 384, 8, 128], P(None, None, ('lat', 'sub')), may hold values from -6 to 6
- damping: float32 [8], P('src'), may hold values from 0.5 to 1
Outputs:
- guess: float32 [8, 24, 384, 8, 128], P(None, None, ('lat', 'sub'), 'src')
- solution: float32 [8, 24, 384, 8, 128], P(None, None, ('lat', 'sub'), 'src')
The draws below stay inside these ranges and needn't reach their ends.
All inputs are finite; a program needn't handle non-finite values.
Results may differ from the reference program's by a relative error of at most 0.0047.
Values sent between devices are 32-bit elements; how exact they have to be, the bound alone decides.
No kernel may reach another device: no remote copies, remote signals or barrier semaphores. Data moves between devices by JAX's collectives and lax.ppermute only.
A program may use at most 64 MiB of HBM per device.

```python
import math
import jax
import jax.numpy as jnp
import numpy as np
from jax import lax

LX = 16
LY = 8
NEV = 32
ITERS = 2
LZ = 8
TIME = 384
PLANE = 128
SOURCES = 8


def levels(stream_key, shape, pieces, low, top_value):
    gain, own = 1.0, jax.random.fold_in(stream_key, 6)
    for dim, parts in pieces:
        heights = jnp.exp(jax.random.uniform(jax.random.fold_in(own, dim), (parts,), jnp.float32, low / len(pieces), top_value / len(pieces)))
        gain = gain * jnp.repeat(heights, shape[dim] // parts).reshape([-1 if axis == dim else 1 for axis in range(len(shape))])
    return gain


def bell_draw(key, shape, deviation, reach, pieces=(), held_as=jnp.bfloat16):
    result = jax.random.normal(key, shape, jnp.float32) * deviation
    if len(pieces) > 0:
        result = levels(key, shape, pieces, -0.22, 0.18) * result
    return jnp.clip(result, min=-reach, max=reach).astype(held_as)


def setup_inputs(seed: int = 0) -> dict:
    arg_keys = jax.random.split(jax.random.key(seed), 6)
    return {
        "sources": bell_draw(arg_keys[0], (SOURCES, 24, TIME, LZ, PLANE), 1.0, 6.0, ((2, 64), (3, 8)), jnp.float32),
        "eigvecs": bell_draw(arg_keys[1], (NEV, 24, TIME, LZ, PLANE), 1.0, 6.0, ((2, 64), (3, 8))),
        "eigvals": jnp.clip(jnp.exp(jax.random.uniform(arg_keys[2], (NEV,), jnp.float32, math.log(0.5), math.log(8.0))), 0.5, 8.0),
        "links": bell_draw(arg_keys[3], (4, 18, TIME, LZ, PLANE), 0.4, 6.0, ((2, 64),), jnp.float32),
        "damping": jnp.clip(0.5 + 0.5 * jax.random.uniform(arg_keys[4], (SOURCES,), jnp.float32) ** levels(arg_keys[4], (SOURCES,), ((0, 8),), -0.2, 0.2), 0.5, 1.0),
    }


HOPPING = 0.12
PRECISE = lax.Precision.HIGHEST
SPIN_BLOCKS = [(np.array([[0.0, 0.0], [0.0, 0.0]]), np.array([[0.0, 1.0], [1.0, 0.0]])), (np.array([[0.0, -1.0], [1.0, 0.0]]), np.zeros((2, 2))), (np.array([[0.0, 0.0], [0.0, 0.0]]), np.array([[1.0, 0.0], [0.0, -1.0]])), (np.eye(2), np.zeros((2, 2)))]

def spin_apply(table_re, table_im, real_part, imag_part):
    matrix_re = jnp.asarray(table_re, jnp.float32)
    matrix_im = jnp.asarray(table_im, jnp.float32)

    def product(matrix, values):
        return jnp.einsum('pq,sq...->sp...', matrix, values, precision=PRECISE)
    return (product(matrix_re, real_part) - product(matrix_im, imag_part), product(matrix_re, imag_part) + product(matrix_im, real_part))

def project(sign, direction, real_part, imag_part):
    table_re, table_im = SPIN_BLOCKS[direction]
    lower_re, lower_im = spin_apply(table_re, table_im, real_part[:, 2:], imag_part[:, 2:])
    return (real_part[:, :2] + sign * lower_re, imag_part[:, :2] + sign * lower_im)

def rebuild(sign, direction, upper_re, upper_im):
    table_re, table_im = SPIN_BLOCKS[direction]
    lower_re, lower_im = spin_apply(table_re.T, -table_im.T, upper_re, upper_im)
    return (jnp.concatenate([upper_re, sign * lower_re], 1), jnp.concatenate([upper_im, sign * lower_im], 1))

def color_mul(links_re, links_im, real_part, imag_part):

    def product(table, values):
        return jnp.einsum('actzw,sbctzw->sbatzw', table, values, precision=PRECISE)
    return (product(links_re, real_part) - product(links_im, imag_part), product(links_re, imag_part) + product(links_im, real_part))

def color_adj(links_re, links_im, real_part, imag_part):

    def product(table, values):
        return jnp.einsum('catzw,sbctzw->sbatzw', table, values, precision=PRECISE)
    return (product(links_re, real_part) + product(links_im, imag_part), product(links_re, imag_part) - product(links_im, real_part))

def link_parts(links, direction):
    extent = links.shape[2:]
    return (links[direction, :9].reshape((3, 3) + extent), links[direction, 9:].reshape((3, 3) + extent))

def neighbour(values, direction, step, antiperiodic):
    if direction == 0:
        shaped = values.reshape(values.shape[:-1] + (LY, LX))
        return jnp.roll(shaped, -step, axis=-1).reshape(values.shape)
    if direction == 1:
        shaped = values.reshape(values.shape[:-1] + (LY, LX))
        return jnp.roll(shaped, -step, axis=-2).reshape(values.shape)
    if direction == 2:
        return jnp.roll(values, -step, axis=-2)
    moved = jnp.roll(values, -step, axis=-3)
    if antiperiodic:
        length = values.shape[-3]
        edge = length - 1 if step > 0 else 0
        factor = jnp.where(jnp.arange(length) == edge, -1.0, 1.0).astype(jnp.float32)
        moved = moved * factor[:, None, None]
    return moved

def split_parts(spinor):
    count = spinor.shape[0]
    extent = spinor.shape[2:]
    return (spinor[:, :12].reshape((count, 4, 3) + extent), spinor[:, 12:].reshape((count, 4, 3) + extent))

def join_parts(real_part, imag_part):
    count = real_part.shape[0]
    extent = real_part.shape[3:]
    return jnp.concatenate([real_part.reshape((count, 12) + extent), imag_part.reshape((count, 12) + extent)], 1)

def wilson(spinor, links):
    real_part, imag_part = split_parts(spinor)
    terms = []
    for direction in range(4):
        links_re, links_im = link_parts(links, direction)
        ahead_re = neighbour(real_part, direction, 1, True)
        ahead_im = neighbour(imag_part, direction, 1, True)
        carried = color_mul(links_re, links_im, ahead_re, ahead_im)
        terms.append(rebuild(-1.0, direction, *project(-1.0, direction, *carried)))
        back_re = neighbour(links_re, direction, -1, False)
        back_im = neighbour(links_im, direction, -1, False)
        behind_re = neighbour(real_part, direction, -1, True)
        behind_im = neighbour(imag_part, direction, -1, True)
        carried = color_adj(back_re, back_im, behind_re, behind_im)
        terms.append(rebuild(1.0, direction, *project(1.0, direction, *carried)))
    total_re, total_im = terms[0]
    for extra in terms[1:]:
        total_re = total_re + extra[0]
        total_im = total_im + extra[1]
    return spinor - HOPPING * join_parts(total_re, total_im)

def reference(sources, eigvecs, eigvals, links, damping):
    count = sources.shape[0]
    flat_src = sources.astype(jnp.bfloat16).reshape(count, 24, -1)
    swapped = jnp.concatenate([flat_src[:, 12:], -flat_src[:, :12]], 1)
    stacked = jnp.concatenate([flat_src, swapped], 0).reshape(2 * count, -1)
    flat_vec = eigvecs.reshape(eigvecs.shape[0], -1)
    correlation = lax.dot_general(flat_vec, stacked, (((1,), (1,)), ((), ())), preferred_element_type=jnp.float32)
    correlation = correlation / math.sqrt(24 * (flat_vec.shape[1] // 24))
    weights = jnp.concatenate([correlation[:, :count].T, correlation[:, count:].T], 0) / eigvals[None, :]
    weights = weights.astype(jnp.bfloat16)
    mixed = jnp.dot(weights, flat_vec, preferred_element_type=jnp.float32)
    middle = mixed.shape[1] // 2
    guess = jnp.concatenate([mixed[:count, :middle] - mixed[count:, middle:], mixed[:count, middle:] + mixed[count:, :middle]], 1).reshape(sources.shape)

    def solve(item):
        source, start, rate = item
        source = source[None]
        iterate = start[None]
        for sweep in range(ITERS):
            iterate = iterate + rate * (source - wilson(iterate, links))
        return iterate[0]
    solution = lax.map(solve, (sources, guess, damping))
    return (guess, solution)
```

```python
import functools
import math

import jax
import jax.numpy as jnp
from jax import lax
from jax.experimental import pallas as pl
from jax.experimental.pallas import tpu as pltpu
from jax.sharding import PartitionSpec as P

LX = 16
ITERS = 2
HOPPING = 0.12

BLOCKS = [
    {(0, 1): 1, (1, 0): 1},
    {(0, 1): 2, (1, 0): 0},
    {(0, 0): 1, (1, 1): 3},
    {(0, 0): 0, (1, 1): 0},
]


def times_power(power, re, im):
    return [
        ((1, re), (1, im)),
        ((-1, im), (1, re)),
        ((-1, re), (-1, im)),
        ((1, im), (-1, re)),
    ][power % 4]


def add_signed(base, sign, value):
    return base + value if sign > 0 else base - value


def project(sign, direction, load):
    half = []
    for row in range(2):
        col, power = next((c, p) for (r, c), p in BLOCKS[direction].items() if r == row)
        colours = []
        for colour in range(3):
            lower_re, lower_im = load(0, 2 + col, colour), load(1, 2 + col, colour)
            (sr, vr), (si, vi) = times_power(power, lower_re, lower_im)
            colours.append(
                (
                    add_signed(load(0, row, colour), sr * sign, vr),
                    add_signed(load(1, row, colour), si * sign, vi),
                )
            )
        half.append(colours)
    return half


def rebuild_into(acc, sign, direction, half):
    def put(key, sgn, value):
        if key in acc:
            acc[key] = add_signed(acc[key], sgn, value)
        else:
            acc[key] = value if sgn > 0 else -value

    for row in range(2):
        for colour in range(3):
            re, im = half[row][colour]
            put((0, row, colour), 1, re)
            put((1, row, colour), 1, im)
    for (row, col), power in BLOCKS[direction].items():
        for colour in range(3):
            re, im = half[row][colour]
            (sr, vr), (si, vi) = times_power(-power, re, im)
            put((0, 2 + col, colour), sr * sign, vr)
            put((1, 2 + col, colour), si * sign, vi)


def colour_mul(link, half, adjoint):
    out = []
    for spin in range(2):
        rows = []
        for row in range(3):
            re = im = None
            for col in range(3):
                lr, li = link[(col, row)] if adjoint else link[(row, col)]
                hr, hi = half[spin][col]
                if adjoint:
                    tr, ti = lr * hr + li * hi, lr * hi - li * hr
                else:
                    tr, ti = lr * hr - li * hi, lr * hi + li * hr
                re = tr if re is None else re + tr
                im = ti if im is None else im + ti
            rows.append((re, im))
        out.append(rows)
    return out


def map_half(fn, half):
    return [[(fn(re), fn(im)) for re, im in rows] for rows in half]


def load_half(load):
    return [[(load(3 * s + c), load(6 + 3 * s + c)) for c in range(3)] for s in range(2)]


def store_half(store, half):
    for s in range(2):
        for c in range(3):
            store(3 * s + c, half[s][c][0])
            store(6 + 3 * s + c, half[s][c][1])


def load_link(links_ref, slices, zdim, direction, t, z):
    def one(comp):
        row = ((direction * 18 + comp) * slices + t) * zdim + z
        return jnp.broadcast_to(links_ref[pl.ds(row, 1), :], (8, 128))

    return {(a, c): (one(3 * a + c), one(9 + 3 * a + c)) for a in range(3) for c in range(3)}


def moved(direction, step):
    def fn(v):
        if direction == 1:
            return pltpu.roll(v, (-step * LX) % 128, 1)
        column = lax.rem(lax.broadcasted_iota(jnp.int32, v.shape, 1), LX)
        border = LX - 1 if step > 0 else 0
        inside = pltpu.roll(v, (-step) % 128, 1)
        wrapped = pltpu.roll(v, (step * (LX - 1)) % 128, 1)
        return jnp.where(column == border, wrapped, inside)

    return fn


def correlation_kernel(eig_ref, src_ref, damp_ref, out_ref, *, nev, slices):
    comps = 24
    sources = 8
    lhs = jnp.concatenate(
        [
            src_ref[pl.ds(t, sources * comps, stride=slices), :].astype(jnp.bfloat16)
            for t in range(slices)
        ],
        axis=1,
    )
    rhs = jnp.concatenate(
        [eig_ref[:, t].reshape(nev * comps, 128) for t in range(slices)], axis=1
    )
    full = lax.dot_general(
        lhs, rhs, (((1,), (1,)), ((), ())), preferred_element_type=jnp.float32
    )
    row = lax.rem(lax.broadcasted_iota(jnp.int32, (sources * comps, 1), 0), comps)
    col = lax.rem(lax.broadcasted_iota(jnp.int32, (1, nev * comps), 1), comps)
    gap = row - col
    straight = jnp.where(gap == 0, full, 0.0)
    crossed = jnp.where(gap == 12, full, 0.0) - jnp.where(gap == -12, full, 0.0)
    straight = straight.reshape(sources, comps, nev * comps).sum(1)
    crossed = crossed.reshape(sources, comps, nev * comps).sum(1)
    first = lax.broadcasted_iota(jnp.int32, (nev * comps, 128), 0)
    lane = lax.broadcasted_iota(jnp.int32, (nev * comps, 128), 1)

    def gather(which):
        start = (lane - which * nev) * comps
        return jnp.where((first >= start) & (first < start + comps), 1.0, 0.0)

    dot = functools.partial(
        jnp.dot, precision=lax.Precision.HIGHEST, preferred_element_type=jnp.float32
    )
    total = dot(straight, gather(0)) + dot(crossed, gather(1))
    mine = lax.axis_index("src")
    holder = (lax.axis_index("lat") == 0) & (lax.axis_index("sub") == 0)
    value = jnp.where(holder, damp_ref[0], 0.0)
    at_row = lax.broadcasted_iota(jnp.int32, (8, 128), 0) == mine
    at_lane = lax.broadcasted_iota(jnp.int32, (8, 128), 1) == 2 * nev
    total = total + jnp.where(at_row & at_lane, value, 0.0)
    out_ref[...] = jnp.broadcast_to(total[None], out_ref.shape)


def emit_halos(load, links_ref, z, t, zup_ref, zdown_ref, slices, zdim):
    up = project(1, 2, load)
    up = colour_mul(load_link(links_ref, slices, zdim, 2, t, z), up, True)
    store_half(lambda i, v: zup_ref.__setitem__((t, i), v), up)
    down = project(-1, 2, load)
    store_half(lambda i, v: zdown_ref.__setitem__((t, i), v), down)


def emit_time_halos(x_ref, links_ref, z, tup_ref, tdown_ref, slices, zdim):
    extent = lax.axis_size(("lat", "sub"))
    place = lax.axis_index(("lat", "sub"))
    up_sign = jnp.where(place == extent - 1, -1.0, 1.0)
    down_sign = jnp.where(place == 0, -1.0, 1.0)
    last = slices - 1
    up = project(1, 3, lambda p, s, c: x_ref[last, 12 * p + 3 * s + c])
    up = colour_mul(load_link(links_ref, slices, zdim, 3, last, z), up, True)
    store_half(lambda i, v: tup_ref.__setitem__(i, v * up_sign), up)
    down = project(-1, 3, lambda p, s, c: x_ref[0, 12 * p + 3 * s + c])
    store_half(lambda i, v: tdown_ref.__setitem__(i, v * down_sign), down)


def guess_kernel(
    part_ref, ev_ref, eig_ref, links_ref,
    guess_ref, x_ref, rate_ref, zup_ref, zdown_ref, tup_ref, tdown_ref,
    *, nev, slices, zdim, norm,
):
    comps = 24
    total = part_ref[0]
    for i in range(1, part_ref.shape[0]):
        total = total + part_ref[i]
    ev = ev_ref[...]
    w_re = ((total[:, :nev] / norm) / ev).astype(jnp.bfloat16)
    w_im = ((total[:, nev : 2 * nev] / norm) / ev).astype(jnp.bfloat16)
    rate_ref[...] = jnp.broadcast_to(total[:, 2 * nev : 2 * nev + 1], (8, 128))
    row = lax.broadcasted_iota(jnp.int32, (nev, nev * comps), 0) * comps
    col = lax.broadcasted_iota(jnp.int32, (nev, nev * comps), 1)
    spread = jnp.where((col >= row) & (col < row + comps), 1.0, 0.0).astype(jnp.bfloat16)
    w_re = jnp.dot(w_re, spread, preferred_element_type=jnp.float32)
    w_im = jnp.dot(w_im, spread, preferred_element_type=jnp.float32)
    comp = lax.rem(lax.broadcasted_iota(jnp.int32, (8, nev * comps), 1), comps)
    blocks = []
    for c in range(comps):
        other, turned = (c + 12, -w_im) if c < 12 else (c - 12, w_im)
        blocks.append(jnp.where(comp == c, w_re, jnp.where(comp == other, turned, 0.0)))
    mix = jnp.concatenate(blocks, axis=0).astype(jnp.bfloat16)
    for t in range(slices):
        res = jnp.dot(
            mix, eig_ref[:, t].reshape(nev * comps, 128), preferred_element_type=jnp.float32
        )
        x_ref[t] = res.reshape(comps, 8, 128)
    z = lax.axis_index("src")

    def step(t, carry):
        for c in range(comps):
            guess_ref[pl.ds(c * slices + t, 8, stride=comps * slices), :] = x_ref[t, c]
        emit_halos(
            lambda p, s, c: x_ref[t, 12 * p + 3 * s + c],
            links_ref, z, t, zup_ref, zdown_ref, slices, zdim,
        )
        return carry

    lax.fori_loop(0, slices, step, 0)
    emit_time_halos(x_ref, links_ref, z, tup_ref, tdown_ref, slices, zdim)


def sweep_slice(x_ref, src_ref, links_ref, rate, from_below, from_above, behind_ref, tin_ref, t, z, slices, zdim):
    load = lambda p, s, c: x_ref[t, 12 * p + 3 * s + c]
    acc = {}
    for direction in range(2):
        link = load_link(links_ref, slices, zdim, direction, t, z)
        ahead = map_half(moved(direction, 1), project(-1, direction, load))
        rebuild_into(acc, -1, direction, colour_mul(link, ahead, False))
        behind = colour_mul(link, project(1, direction, load), True)
        rebuild_into(acc, 1, direction, map_half(moved(direction, -1), behind))
    link = load_link(links_ref, slices, zdim, 2, t, z)
    ahead = load_half(lambda i: from_above[t, i])
    rebuild_into(acc, -1, 2, colour_mul(link, ahead, False))
    rebuild_into(acc, 1, 2, load_half(lambda i: from_below[t, i]))
    link = load_link(links_ref, slices, zdim, 3, t, z)
    last = t == slices - 1
    following = jnp.minimum(t + 1, slices - 1)
    ahead = project(-1, 3, lambda p, s, c: x_ref[following, 12 * p + 3 * s + c])
    edge = load_half(lambda i: tin_ref[i])
    ahead = [
        [
            tuple(jnp.where(last, e, a) for a, e in zip(ahead[s][c], edge[s][c]))
            for c in range(3)
        ]
        for s in range(2)
    ]
    rebuild_into(acc, -1, 3, colour_mul(link, ahead, False))
    rebuild_into(acc, 1, 3, load_half(lambda i: behind_ref[i]))
    up = colour_mul(link, project(1, 3, load), True)
    store_half(lambda i, v: behind_ref.__setitem__(i, v), up)
    out = {}
    for (p, s, c), hop in acc.items():
        comp = 12 * p + 3 * s + c
        source = src_ref[pl.ds(comp * slices + t, 8, stride=24 * slices), :]
        value = load(p, s, c)
        out[(p, s, c)] = value + rate * (source - (value - HOPPING * hop))
    return out


def sweep_kernel(
    x_ref, src_ref, links_ref, rate_ref, below_ref, above_ref, tbelow_ref, tabove_ref, *refs,
    slices, zdim, final,
):
    z = lax.axis_index("src")
    behind_ref = refs[-1]
    behind_ref[...] = tbelow_ref[...]

    def step(t, carry):
        rate = rate_ref[...]
        new = sweep_slice(
            x_ref, src_ref, links_ref, rate, below_ref, above_ref, behind_ref, tabove_ref,
            t, z, slices, zdim,
        )
        for (p, s, c), value in new.items():
            comp = 12 * p + 3 * s + c
            if final:
                refs[0][pl.ds(comp * slices + t, 8, stride=24 * slices), :] = value
            else:
                refs[0][t, comp] = value
        if not final:
            emit_halos(
                lambda p, s, c: new[(p, s, c)],
                links_ref, z, t, refs[1], refs[2], slices, zdim,
            )
        return carry

    lax.fori_loop(0, slices, step, 0)
    if not final:
        emit_time_halos(refs[0], links_ref, z, refs[3], refs[4], slices, zdim)


def vmem():
    return pl.BlockSpec(memory_space=pltpu.VMEM)


def call(kernel, outs, name, ins, flops, smem=(), scratch=()):
    return pl.pallas_call(
        kernel,
        out_shape=outs,
        in_specs=[
            pl.BlockSpec(memory_space=pltpu.SMEM) if i in smem else vmem() for i in range(ins)
        ],
        out_specs=jax.tree.map(lambda _: vmem(), outs),
        scratch_shapes=list(scratch),
        name=name,
        compiler_params=pltpu.CompilerParams(vmem_limit_bytes=24 << 20),
        cost_estimate=pl.CostEstimate(
            flops=flops, bytes_accessed=3_000_000, transcendentals=0
        ),
    )


def shards(sources, eigvecs, eigvals, links, damping):
    count, comps, slices = sources.shape[:3]
    nev = eigvecs.shape[0]
    zdim = links.shape[3]
    devices = lax.axis_size(("src", "lat", "sub"))
    norm = math.sqrt(comps * slices * 128 * devices)
    f32 = jnp.float32

    src = sources.reshape(count * comps * slices, 128)
    eig = eigvecs.transpose(0, 2, 3, 1, 4).reshape(nev, slices, comps, 128)
    flat_links = links.reshape(4 * 18 * slices * zdim, 128)

    shape = lambda *dims: jax.ShapeDtypeStruct(dims, f32)
    lat, rest = lax.axis_size("lat"), lax.axis_size(("sub", "src"))
    partial = call(
        functools.partial(correlation_kernel, nev=nev, slices=slices),
        shape(lat, 8, 128), "correlation", 3, 226_000_000, smem=(2,),
    )(eig, src, damping)
    partial = lax.all_to_all(partial, "lat", 0, 0, tiled=True)
    partial = jnp.broadcast_to(partial.sum(0)[None], (rest, 8, 128))
    partial = lax.all_to_all(partial, ("sub", "src"), 0, 0, tiled=True)

    field = shape(slices, comps, 8, 128)
    halos = (shape(slices, 12, 8, 128),) * 2 + (shape(12, 8, 128),) * 2
    flat = shape(count * comps * slices, 128)
    guess, x, rate, *send = call(
        functools.partial(guess_kernel, nev=nev, slices=slices, zdim=zdim, norm=norm),
        (flat, field, shape(8, 128)) + halos, "guess", 4, 226_000_000,
    )(partial, eigvals.reshape(1, nev), eig, flat_links)

    def exchange(send):
        zup, zdown, tup, tdown = send
        nz, nt = lax.axis_size("src"), lax.axis_size(("lat", "sub"))
        up = lambda n: [(i, (i + 1) % n) for i in range(n)]
        down = lambda n: [((i + 1) % n, i) for i in range(n)]
        return (
            lax.ppermute(zup, "src", up(nz)),
            lax.ppermute(zdown, "src", down(nz)),
            lax.ppermute(tup, ("lat", "sub"), up(nt)),
            lax.ppermute(tdown, ("lat", "sub"), down(nt)),
        )

    for sweep in range(ITERS):
        final = sweep == ITERS - 1
        got = exchange(send)
        outs = flat if final else (field,) + halos
        res = call(
            functools.partial(sweep_kernel, slices=slices, zdim=zdim, final=final),
            outs, "last_sweep" if final else "sweep", 8, 10_000_000,
            scratch=[pltpu.VMEM((12, 8, 128), f32)],
        )(x, src, flat_links, rate, *got)
        if final:
            x = res
        else:
            x, *send = res
    return (guess.reshape(sources.shape), x.reshape(sources.shape))


def solution(mesh):
    return jax.shard_map(
        shards,
        mesh=mesh,
        in_specs=(
            P(None, None, ("lat", "sub"), "src", None),
            P(None, None, ("lat", "sub"), "src", None),
            P(),
            P(None, None, ("lat", "sub"), None, None),
            P("src"),
        ),
        out_specs=(
            P(None, None, ("lat", "sub"), "src", None),
            P(None, None, ("lat", "sub"), "src", None),
        ),
        check_vma=False,
    )
```

```python
import functools
import math

import jax
import jax.numpy as jnp
from jax import lax
from jax.experimental import pallas as pl
from jax.experimental.pallas import tpu as pltpu
from jax.sharding import PartitionSpec as P

LX = 16
ITERS = 2
HOPPING = 0.12

BLOCKS = [
    {(0, 1): 1, (1, 0): 1},
    {(0, 1): 2, (1, 0): 0},
    {(0, 0): 1, (1, 1): 3},
    {(0, 0): 0, (1, 1): 0},
]


def times_power(power, re, im):
    return [
        ((1, re), (1, im)),
        ((-1, im), (1, re)),
        ((-1, re), (-1, im)),
        ((1, im), (-1, re)),
    ][power % 4]


def add_signed(base, sign, value):
    return base + value if sign > 0 else base - value


def project(sign, direction, load):
    half = []
    for row in range(2):
        col, power = next((c, p) for (r, c), p in BLOCKS[direction].items() if r == row)
        colours = []
        for colour in range(3):
            lower_re, lower_im = load(0, 2 + col, colour), load(1, 2 + col, colour)
            (sr, vr), (si, vi) = times_power(power, lower_re, lower_im)
            colours.append(
                (
                    add_signed(load(0, row, colour), sr * sign, vr),
                    add_signed(load(1, row, colour), si * sign, vi),
                )
            )
        half.append(colours)
    return half


def rebuild_into(acc, sign, direction, half):
    def put(key, sgn, value):
        if key in acc:
            acc[key] = add_signed(acc[key], sgn, value)
        else:
            acc[key] = value if sgn > 0 else -value

    for row in range(2):
        for colour in range(3):
            re, im = half[row][colour]
            put((0, row, colour), 1, re)
            put((1, row, colour), 1, im)
    for (row, col), power in BLOCKS[direction].items():
        for colour in range(3):
            re, im = half[row][colour]
            (sr, vr), (si, vi) = times_power(-power, re, im)
            put((0, 2 + col, colour), sr * sign, vr)
            put((1, 2 + col, colour), si * sign, vi)


def colour_mul(link, half, adjoint):
    out = []
    for spin in range(2):
        rows = []
        for row in range(3):
            re = im = None
            for col in range(3):
                lr, li = link[(col, row)] if adjoint else link[(row, col)]
                hr, hi = half[spin][col]
                if adjoint:
                    tr, ti = lr * hr + li * hi, lr * hi - li * hr
                else:
                    tr, ti = lr * hr - li * hi, lr * hi + li * hr
                re = tr if re is None else re + tr
                im = ti if im is None else im + ti
            rows.append((re, im))
        out.append(rows)
    return out


def map_half(fn, half):
    return [[(fn(re), fn(im)) for re, im in rows] for rows in half]


def load_half(load):
    return [[(load(3 * s + c), load(6 + 3 * s + c)) for c in range(3)] for s in range(2)]


def store_half(store, half):
    for s in range(2):
        for c in range(3):
            store(3 * s + c, half[s][c][0])
            store(6 + 3 * s + c, half[s][c][1])


def load_link(links_ref, slices, direction, t):
    def one(comp):
        row = (direction * 18 + comp) * slices + t
        return jnp.broadcast_to(links_ref[pl.ds(row, 1), :], (8, 128))

    return {(a, c): (one(3 * a + c), one(9 + 3 * a + c)) for a in range(3) for c in range(3)}


def moved(direction, step):
    def fn(v):
        if direction == 1:
            return pltpu.roll(v, (-step * LX) % 128, 1)
        column = lax.rem(lax.broadcasted_iota(jnp.int32, v.shape, 1), LX)
        border = LX - 1 if step > 0 else 0
        inside = pltpu.roll(v, (-step) % 128, 1)
        wrapped = pltpu.roll(v, (step * (LX - 1)) % 128, 1)
        return jnp.where(column == border, wrapped, inside)

    return fn


def correlation_kernel(
    eig_hbm, src_hbm, links_hbm, damp_ref, out_ref, eig_ref, links_ref, src_ref, sems, *, nev, slices
):
    comps = 24
    sources = 8
    rows = sources * comps * slices // 2
    src_copies = [
        pltpu.make_async_copy(
            src_hbm.at[pl.ds(i * rows, rows)], src_ref.at[pl.ds(i * rows, rows)], sems.at[slices + i]
        )
        for i in range(2)
    ]
    eig_copies = [
        pltpu.make_async_copy(eig_hbm.at[:, t], eig_ref.at[:, t], sems.at[t]) for t in range(slices)
    ]
    links_copy = pltpu.make_async_copy(
        links_hbm.at[:, lax.axis_index("src")], links_ref, sems.at[slices + 2]
    )
    for copy in src_copies + eig_copies + [links_copy]:
        copy.start()
    for copy in src_copies:
        copy.wait()
    full = jnp.zeros((sources * comps, nev * comps), jnp.float32)
    for t in range(0, slices, 2):
        lhs = [
            src_ref[pl.ds(u, sources * comps, stride=slices), :].astype(jnp.bfloat16)
            for u in (t, t + 1)
        ]
        eig_copies[t].wait()
        eig_copies[t + 1].wait()
        rhs = [eig_ref[:, u].reshape(nev * comps, 128) for u in (t, t + 1)]
        full = full + lax.dot_general(
            jnp.concatenate(lhs, axis=1), jnp.concatenate(rhs, axis=1),
            (((1,), (1,)), ((), ())), preferred_element_type=jnp.float32,
        )
    row = lax.rem(lax.broadcasted_iota(jnp.int32, (sources * comps, 1), 0), comps)
    col = lax.rem(lax.broadcasted_iota(jnp.int32, (1, nev * comps), 1), comps)
    gap = row - col
    straight = jnp.where(gap == 0, full, 0.0)
    crossed = jnp.where(gap == 12, full, 0.0) - jnp.where(gap == -12, full, 0.0)
    straight = straight.reshape(sources, comps, nev * comps).sum(1)
    crossed = crossed.reshape(sources, comps, nev * comps).sum(1)
    first = lax.broadcasted_iota(jnp.int32, (nev * comps, 128), 0)
    lane = lax.broadcasted_iota(jnp.int32, (nev * comps, 128), 1)

    def gather(which):
        start = (lane - which * nev) * comps
        return jnp.where((first >= start) & (first < start + comps), 1.0, 0.0)

    dot = functools.partial(
        jnp.dot, precision=lax.Precision.HIGHEST, preferred_element_type=jnp.float32
    )
    total = dot(straight, gather(0)) + dot(crossed, gather(1))
    links_copy.wait()
    holder = (lax.axis_index("lat") == 0) & (lax.axis_index("sub") == 0)
    value = jnp.where(holder, damp_ref[0], 0.0)
    at_row = lax.broadcasted_iota(jnp.int32, (8, 128), 0) == lax.axis_index("src")
    at_lane = lax.broadcasted_iota(jnp.int32, (8, 128), 1) == 2 * nev
    total = total + jnp.where(at_row & at_lane, value, 0.0)
    out_ref[...] = jnp.broadcast_to(total[None], out_ref.shape)


def choose(flag, half_true, half_false):
    return [
        [
            tuple(jnp.where(flag, a, b) for a, b in zip(half_true[s][c], half_false[s][c]))
            for c in range(3)
        ]
        for s in range(2)
    ]


def z_even():
    return lax.rem(lax.axis_index("src"), 2) == 0


def t_place():
    place = lax.axis_index(("lat", "sub"))
    return place, lax.rem(place, 2) == 0


def emit_halos(load, links_ref, t, near_ref, far_ref, slices):
    even = z_even()
    up = project(1, 2, load)
    up = colour_mul(load_link(links_ref, slices, 2, t), up, True)
    down = project(-1, 2, load)
    store_half(lambda i, v: near_ref.__setitem__((t, i), v), choose(even, up, down))
    store_half(lambda i, v: far_ref.__setitem__((t, i), v), choose(even, down, up))


def emit_time_halos(x_ref, links_ref, near_ref, far_ref, slices):
    place, even = t_place()
    extent = lax.axis_size(("lat", "sub"))
    up_sign = jnp.where(place == extent - 1, -1.0, 1.0)
    down_sign = jnp.where(place == 0, -1.0, 1.0)
    last = slices - 1
    up = project(1, 3, lambda p, s, c: x_ref[last, 12 * p + 3 * s + c])
    up = colour_mul(load_link(links_ref, slices, 3, last), up, True)
    up = map_half(lambda v: v * up_sign, up)
    down = project(-1, 3, lambda p, s, c: x_ref[0, 12 * p + 3 * s + c])
    down = map_half(lambda v: v * down_sign, down)
    store_half(lambda i, v: near_ref.__setitem__(i, v), choose(even, up, down))
    store_half(lambda i, v: far_ref.__setitem__(i, v), choose(even, down, up))


def guess_kernel(
    part_ref, ev_ref, eig_ref, links_ref, x_ref, rate_ref, znear_ref, zfar_ref, tnear_ref, tfar_ref,
    *, nev, slices, norm,
):
    comps = 24
    total = part_ref[0]
    for i in range(1, part_ref.shape[0]):
        total = total + part_ref[i]
    ev = ev_ref[...]
    w_re = ((total[:, :nev] / norm) / ev).astype(jnp.bfloat16)
    w_im = ((total[:, nev : 2 * nev] / norm) / ev).astype(jnp.bfloat16)
    rate_ref[...] = jnp.broadcast_to(total[:, 2 * nev : 2 * nev + 1], (8, 128))
    row = lax.broadcasted_iota(jnp.int32, (nev, nev * comps), 0) * comps
    col = lax.broadcasted_iota(jnp.int32, (nev, nev * comps), 1)
    spread = jnp.where((col >= row) & (col < row + comps), 1.0, 0.0).astype(jnp.bfloat16)
    w_re = jnp.dot(w_re, spread, preferred_element_type=jnp.float32)
    w_im = jnp.dot(w_im, spread, preferred_element_type=jnp.float32)
    comp = lax.rem(lax.broadcasted_iota(jnp.int32, (8, nev * comps), 1), comps)
    blocks = []
    for c in range(comps):
        other, turned = (c + 12, -w_im) if c < 12 else (c - 12, w_im)
        blocks.append(jnp.where(comp == c, w_re, jnp.where(comp == other, turned, 0.0)))
    mix = jnp.concatenate(blocks, axis=0).astype(jnp.bfloat16)
    for t in range(slices):
        res = jnp.dot(
            mix, eig_ref[:, t].reshape(nev * comps, 128), preferred_element_type=jnp.float32
        )
        x_ref[t] = res.reshape(comps, 8, 128)

    def step(t, carry):
        emit_halos(
            lambda p, s, c: x_ref[t, 12 * p + 3 * s + c],
            links_ref, t, znear_ref, zfar_ref, slices,
        )
        return carry

    lax.fori_loop(0, slices, step, 0)
    emit_time_halos(x_ref, links_ref, tnear_ref, tfar_ref, slices)


def local_kernel(x_ref, src_ref, links_ref, rate_ref, *refs, slices, keep):
    y_ref, behind_ref = refs[0], refs[-1]
    behind_ref[...] = jnp.zeros_like(behind_ref)

    def step(t, carry):
        load = lambda p, s, c: x_ref[t, 12 * p + 3 * s + c]
        acc = {}
        for direction in range(2):
            link = load_link(links_ref, slices, direction, t)
            ahead = map_half(moved(direction, 1), project(-1, direction, load))
            rebuild_into(acc, -1, direction, colour_mul(link, ahead, False))
            behind = colour_mul(link, project(1, direction, load), True)
            rebuild_into(acc, 1, direction, map_half(moved(direction, -1), behind))
        link = load_link(links_ref, slices, 3, t)
        inside = jnp.where(t == slices - 1, 0.0, 1.0)
        following = jnp.minimum(t + 1, slices - 1)
        ahead = project(-1, 3, lambda p, s, c: x_ref[following, 12 * p + 3 * s + c])
        ahead = map_half(lambda v: v * inside, ahead)
        rebuild_into(acc, -1, 3, colour_mul(link, ahead, False))
        rebuild_into(acc, 1, 3, load_half(lambda i: behind_ref[i]))
        up = colour_mul(link, project(1, 3, load), True)
        store_half(lambda i, v: behind_ref.__setitem__(i, v), up)
        rate = rate_ref[...]
        for (p, s, c), hop in acc.items():
            comp = 12 * p + 3 * s + c
            where = pl.ds(comp * slices + t, 8, stride=24 * slices)
            value = load(p, s, c)
            y_ref[t, comp] = value + rate * (src_ref[where, :] - (value - HOPPING * hop))
            if keep:
                refs[1][where, :] = value
        return carry

    lax.fori_loop(0, slices, step, 0)


def halo_kernel(
    y_ref, links_ref, rate_ref, znear_ref, zfar_ref, tnear_ref, tfar_ref, *refs, slices, final
):
    above_near = z_even()
    _, t_even = t_place()
    edge_ref = refs[-1]
    last = slices - 1
    near, far = (load_half(lambda i, ref=ref: ref[i]) for ref in (tnear_ref, tfar_ref))
    link = load_link(links_ref, slices, 3, last)
    above = colour_mul(link, choose(t_even, near, far), False)
    store_half(lambda i, v: edge_ref.__setitem__((0, i), v), above)
    store_half(lambda i, v: edge_ref.__setitem__((1, i), v), choose(t_even, far, near))

    def step(t, carry):
        acc = {}
        near, far = (load_half(lambda i, ref=ref: ref[t, i]) for ref in (znear_ref, zfar_ref))
        link = load_link(links_ref, slices, 2, t)
        rebuild_into(acc, -1, 2, colour_mul(link, choose(above_near, near, far), False))
        rebuild_into(acc, 1, 2, choose(above_near, far, near))
        top, bottom = (jnp.where(t == edge, 1.0, 0.0) for edge in (last, 0))
        rebuild_into(acc, -1, 3, map_half(lambda v: v * top, load_half(lambda i: edge_ref[0, i])))
        rebuild_into(acc, 1, 3, map_half(lambda v: v * bottom, load_half(lambda i: edge_ref[1, i])))
        rate = rate_ref[...] * HOPPING
        new = {}
        for (p, s, c), hop in acc.items():
            comp = 12 * p + 3 * s + c
            value = y_ref[t, comp] + rate * hop
            new[(p, s, c)] = value
            if final:
                refs[0][pl.ds(comp * slices + t, 8, stride=24 * slices), :] = value
            else:
                refs[0][t, comp] = value
        if not final:
            emit_halos(
                lambda p, s, c: new[(p, s, c)], links_ref, t, refs[1], refs[2], slices
            )
        return carry

    lax.fori_loop(0, slices, step, 0)
    if not final:
        emit_time_halos(refs[0], links_ref, refs[3], refs[4], slices)


def call(kernel, outs, ins, flops, hbm=(), smem=(), scratch=()):
    space = lambda i: pltpu.HBM if i in hbm else pltpu.SMEM if i in smem else pltpu.VMEM
    return pl.pallas_call(
        kernel,
        out_shape=outs,
        in_specs=[pl.BlockSpec(memory_space=space(i)) for i in range(ins)],
        out_specs=jax.tree.map(lambda _: pl.BlockSpec(memory_space=pltpu.VMEM), outs),
        scratch_shapes=list(scratch),
        compiler_params=pltpu.CompilerParams(vmem_limit_bytes=24 << 20),
        cost_estimate=pl.CostEstimate(
            flops=flops, bytes_accessed=3_000_000, transcendentals=0
        ),
    )


def exchange(send):
    znear, zfar, tnear, tfar = send
    nz, nt = lax.axis_size("src"), lax.axis_size(("lat", "sub"))
    near = lambda n: [(i, i ^ 1) for i in range(n)]
    far = lambda n: [(i, (i + 1 if i % 2 else i - 1) % n) for i in range(n)]

    return (
        lax.ppermute(znear, "src", near(nz)),
        lax.ppermute(zfar, "src", far(nz)),
        lax.ppermute(tnear, ("lat", "sub"), near(nt)),
        lax.ppermute(tfar, ("lat", "sub"), far(nt)),
    )


def shards(sources, eigvecs, eigvals, links, damping):
    count, comps, slices = sources.shape[:3]
    nev = eigvecs.shape[0]
    zdim = links.shape[3]
    devices = lax.axis_size(("src", "lat", "sub"))
    norm = math.sqrt(comps * slices * 128 * devices)
    f32 = jnp.float32

    src = sources.reshape(count * comps * slices, 128)
    eig = eigvecs.transpose(0, 2, 3, 1, 4).reshape(nev, slices, comps, 128)

    shape = lambda *dims: jax.ShapeDtypeStruct(dims, f32)
    lat, rest = lax.axis_size("lat"), lax.axis_size(("sub", "src"))
    links = links.reshape(4 * 18 * slices, zdim, 128)
    partial, eig, flat_links = call(
        functools.partial(correlation_kernel, nev=nev, slices=slices),
        (
            shape(lat, 8, 128),
            jax.ShapeDtypeStruct(eig.shape, eig.dtype),
            shape(4 * 18 * slices, 128),
        ),
        4, 226_000_000, hbm=(0, 1, 2), smem=(3,),
        scratch=[
            pltpu.VMEM(src.shape, f32),
            pltpu.SemaphoreType.DMA((slices + 3,)),
        ],
    )(*(pltpu.with_memory_space_constraint(x, pltpu.HBM) for x in (eig, src, links)), damping)
    partial = lax.all_to_all(partial, "lat", 0, 0, tiled=True)
    partial = jnp.broadcast_to(partial.sum(0)[None], (rest, 8, 128))
    partial = lax.all_to_all(partial, ("sub", "src"), 0, 0, tiled=True)

    field = shape(slices, comps, 8, 128)
    halos = (shape(slices, 12, 8, 128),) * 2 + (shape(12, 8, 128),) * 2
    flat = shape(count * comps * slices, 128)
    x, rate, *send = call(
        functools.partial(guess_kernel, nev=nev, slices=slices, norm=norm),
        (field, shape(8, 128)) + halos, 4, 226_000_000,
    )(partial, eigvals.reshape(1, nev), eig, flat_links)

    guess = None
    for sweep in range(ITERS):
        final = sweep == ITERS - 1
        keep = sweep == 0
        got = exchange(send)
        y, *kept = call(
            functools.partial(local_kernel, slices=slices, keep=keep),
            (field,) + ((flat,) if keep else ()), 4, 10_000_000,
            scratch=[pltpu.VMEM((12, 8, 128), f32)],
        )(x, src, flat_links, rate)
        if keep:
            guess = kept[0]
        outs = flat if final else (field,) + halos
        res = call(
            functools.partial(halo_kernel, slices=slices, final=final),
            outs, 7, 5_000_000,
            scratch=[pltpu.VMEM((2, 12, 8, 128), f32)],
        )(y, flat_links, rate, *got)
        if final:
            x = res
        else:
            x, *send = res
    return (guess.reshape(sources.shape), x.reshape(sources.shape))


def solution(mesh):
    return jax.shard_map(
        shards,
        mesh=mesh,
        in_specs=(
            P(None, None, ("lat", "sub"), "src", None),
            P(None, None, ("lat", "sub"), "src", None),
            P(),
            P(None, None, ("lat", "sub"), None, None),
            P("src"),
        ),
        out_specs=(
            P(None, None, ("lat", "sub"), "src", None),
            P(None, None, ("lat", "sub"), "src", None),
        ),
        check_vma=False,
    )
```

```python
import functools
import math

import jax
import jax.numpy as jnp
from jax import lax
from jax.experimental import pallas as pl
from jax.experimental.pallas import tpu as pltpu
from jax.sharding import PartitionSpec as P

LX = 16
ITERS = 2
HOPPING = 0.12

BLOCKS = [
    {(0, 1): 1, (1, 0): 1},
    {(0, 1): 2, (1, 0): 0},
    {(0, 0): 1, (1, 1): 3},
    {(0, 0): 0, (1, 1): 0},
]


def times_power(power, re, im):
    return [
        ((1, re), (1, im)),
        ((-1, im), (1, re)),
        ((-1, re), (-1, im)),
        ((1, im), (-1, re)),
    ][power % 4]


def add_signed(base, sign, value):
    return base + value if sign > 0 else base - value


def project(sign, direction, load):
    half = []
    for row in range(2):
        col, power = next((c, p) for (r, c), p in BLOCKS[direction].items() if r == row)
        colours = []
        for colour in range(3):
            lower_re, lower_im = load(0, 2 + col, colour), load(1, 2 + col, colour)
            (sr, vr), (si, vi) = times_power(power, lower_re, lower_im)
            colours.append(
                (
                    add_signed(load(0, row, colour), sr * sign, vr),
                    add_signed(load(1, row, colour), si * sign, vi),
                )
            )
        half.append(colours)
    return half


def rebuild_into(acc, sign, direction, half):
    def put(key, sgn, value):
        if key in acc:
            acc[key] = add_signed(acc[key], sgn, value)
        else:
            acc[key] = value if sgn > 0 else -value

    for row in range(2):
        for colour in range(3):
            re, im = half[row][colour]
            put((0, row, colour), 1, re)
            put((1, row, colour), 1, im)
    for (row, col), power in BLOCKS[direction].items():
        for colour in range(3):
            re, im = half[row][colour]
            (sr, vr), (si, vi) = times_power(-power, re, im)
            put((0, 2 + col, colour), sr * sign, vr)
            put((1, 2 + col, colour), si * sign, vi)


def colour_mul(link, half, adjoint):
    out = []
    for spin in range(2):
        rows = []
        for row in range(3):
            re = im = None
            for col in range(3):
                lr, li = link[(col, row)] if adjoint else link[(row, col)]
                hr, hi = half[spin][col]
                if adjoint:
                    tr, ti = lr * hr + li * hi, lr * hi - li * hr
                else:
                    tr, ti = lr * hr - li * hi, lr * hi + li * hr
                re = tr if re is None else re + tr
                im = ti if im is None else im + ti
            rows.append((re, im))
        out.append(rows)
    return out


def map_half(fn, half):
    return [[(fn(re), fn(im)) for re, im in rows] for rows in half]


def load_half(load):
    return [[(load(3 * s + c), load(6 + 3 * s + c)) for c in range(3)] for s in range(2)]


def store_half(store, half):
    for s in range(2):
        for c in range(3):
            store(3 * s + c, half[s][c][0])
            store(6 + 3 * s + c, half[s][c][1])


def load_link(links_ref, slices, direction, t):
    def one(comp):
        row = (direction * 18 + comp) * slices + t
        return jnp.broadcast_to(links_ref[pl.ds(row, 1), :], (8, 128))

    return {(a, c): (one(3 * a + c), one(9 + 3 * a + c)) for a in range(3) for c in range(3)}


def moved(direction, step):
    def fn(v):
        if direction == 1:
            return pltpu.roll(v, (-step * LX) % 128, 1)
        column = lax.rem(lax.broadcasted_iota(jnp.int32, v.shape, 1), LX)
        border = LX - 1 if step > 0 else 0
        inside = pltpu.roll(v, (-step) % 128, 1)
        wrapped = pltpu.roll(v, (step * (LX - 1)) % 128, 1)
        return jnp.where(column == border, wrapped, inside)

    return fn


def correlation_kernel(
    eig_hbm, src_hbm, out_ref, eig_ref, slot_ref, src_ref, sems, *, nev, slices
):
    comps = 24
    sources = 8
    rows = sources * comps * slices // 2
    src_copies = [
        pltpu.make_async_copy(
            src_hbm.at[pl.ds(i * rows, rows)], src_ref.at[pl.ds(i * rows, rows)], sems.at[slices + i]
        )
        for i in range(2)
    ]
    eig_copies = [
        pltpu.make_async_copy(eig_hbm.at[:, t], eig_ref.at[:, t], sems.at[t]) for t in range(slices)
    ]
    for copy in src_copies + eig_copies:
        copy.start()
    for copy in src_copies:
        copy.wait()
    full = jnp.zeros((sources * comps, nev * comps), jnp.float32)
    for t in range(0, slices, 2):
        lhs = [
            src_ref[pl.ds(u, sources * comps, stride=slices), :].astype(jnp.bfloat16)
            for u in (t, t + 1)
        ]
        eig_copies[t].wait()
        eig_copies[t + 1].wait()
        rhs = [eig_ref[:, u].reshape(nev * comps, 128) for u in (t, t + 1)]
        full = full + lax.dot_general(
            jnp.concatenate(lhs, axis=1), jnp.concatenate(rhs, axis=1),
            (((1,), (1,)), ((), ())), preferred_element_type=jnp.float32,
        )
    row = lax.rem(lax.broadcasted_iota(jnp.int32, (sources * comps, 1), 0), comps)
    col = lax.rem(lax.broadcasted_iota(jnp.int32, (1, nev * comps), 1), comps)
    gap = row - col
    straight = jnp.where(gap == 0, full, 0.0)
    crossed = jnp.where(gap == 12, full, 0.0) - jnp.where(gap == -12, full, 0.0)
    straight = straight.reshape(sources, comps, nev * comps).sum(1)
    crossed = crossed.reshape(sources, comps, nev * comps).sum(1)
    first = lax.broadcasted_iota(jnp.int32, (nev * comps, 128), 0)
    lane = lax.broadcasted_iota(jnp.int32, (nev * comps, 128), 1)

    def gather(which):
        start = (lane - which * nev) * comps
        return jnp.where((first >= start) & (first < start + comps), 1.0, 0.0)

    dot = functools.partial(
        jnp.dot, precision=lax.Precision.HIGHEST, preferred_element_type=jnp.float32
    )
    total = dot(straight, gather(0)) + dot(crossed, gather(1))
    out_ref[...] = jnp.broadcast_to(total[None], out_ref.shape)
    at_row = lax.broadcasted_iota(jnp.int32, (8, 128), 0) == lax.axis_index("src")
    at_lane = lax.broadcasted_iota(jnp.int32, (8, 128), 1) == 2 * nev
    holder = jnp.where(lax.axis_index("sub") == 0, 1.0, 0.0)
    slot_ref[...] = jnp.where(at_row & at_lane, holder, 0.0)


def slab_kernel(links_hbm, links_ref, sem):
    copy = pltpu.make_async_copy(links_hbm.at[:, lax.axis_index("src")], links_ref, sem)
    copy.start()
    copy.wait()


def choose(flag, half_true, half_false):
    return [
        [
            tuple(jnp.where(flag, a, b) for a, b in zip(half_true[s][c], half_false[s][c]))
            for c in range(3)
        ]
        for s in range(2)
    ]


def z_even():
    return lax.rem(lax.axis_index("src"), 2) == 0


def t_place():
    place = lax.axis_index(("lat", "sub"))
    return place, lax.rem(place, 2) == 0


def emit_halos(load, links_ref, t, near_ref, far_ref, slices):
    even = z_even()
    up = project(1, 2, load)
    up = colour_mul(load_link(links_ref, slices, 2, t), up, True)
    down = project(-1, 2, load)
    store_half(lambda i, v: near_ref.__setitem__((t, i), v), choose(even, up, down))
    store_half(lambda i, v: far_ref.__setitem__((t, i), v), choose(even, down, up))


def emit_time_halos(x_ref, links_ref, near_ref, far_ref, slices):
    place, even = t_place()
    extent = lax.axis_size(("lat", "sub"))
    up_sign = jnp.where(place == extent - 1, -1.0, 1.0)
    down_sign = jnp.where(place == 0, -1.0, 1.0)
    last = slices - 1
    up = project(1, 3, lambda p, s, c: x_ref[last, 12 * p + 3 * s + c])
    up = colour_mul(load_link(links_ref, slices, 3, last), up, True)
    up = map_half(lambda v: v * up_sign, up)
    down = project(-1, 3, lambda p, s, c: x_ref[0, 12 * p + 3 * s + c])
    down = map_half(lambda v: v * down_sign, down)
    store_half(lambda i, v: near_ref.__setitem__(i, v), choose(even, up, down))
    store_half(lambda i, v: far_ref.__setitem__(i, v), choose(even, down, up))


def guess_kernel(
    part_ref, ev_ref, eig_ref, links_ref, x_ref, rate_ref, znear_ref, zfar_ref, tnear_ref, tfar_ref,
    *, nev, slices, norm,
):
    comps = 24
    total = part_ref[0]
    for i in range(1, part_ref.shape[0]):
        total = total + part_ref[i]
    ev = ev_ref[...]
    w_re = ((total[:, :nev] / norm) / ev).astype(jnp.bfloat16)
    w_im = ((total[:, nev : 2 * nev] / norm) / ev).astype(jnp.bfloat16)
    rate_ref[...] = jnp.broadcast_to(total[:, 2 * nev : 2 * nev + 1], (8, 128))
    row = lax.broadcasted_iota(jnp.int32, (nev, nev * comps), 0) * comps
    col = lax.broadcasted_iota(jnp.int32, (nev, nev * comps), 1)
    spread = jnp.where((col >= row) & (col < row + comps), 1.0, 0.0).astype(jnp.bfloat16)
    w_re = jnp.dot(w_re, spread, preferred_element_type=jnp.float32)
    w_im = jnp.dot(w_im, spread, preferred_element_type=jnp.float32)
    comp = lax.rem(lax.broadcasted_iota(jnp.int32, (8, nev * comps), 1), comps)
    blocks = []
    for c in range(comps):
        other, turned = (c + 12, -w_im) if c < 12 else (c - 12, w_im)
        blocks.append(jnp.where(comp == c, w_re, jnp.where(comp == other, turned, 0.0)))
    mix = jnp.concatenate(blocks, axis=0).astype(jnp.bfloat16)
    for t in range(slices):
        res = jnp.dot(
            mix, eig_ref[:, t].reshape(nev * comps, 128), preferred_element_type=jnp.float32
        )
        x_ref[t] = res.reshape(comps, 8, 128)

    def step(t, carry):
        emit_halos(
            lambda p, s, c: x_ref[t, 12 * p + 3 * s + c],
            links_ref, t, znear_ref, zfar_ref, slices,
        )
        return carry

    lax.fori_loop(0, slices, step, 0)
    emit_time_halos(x_ref, links_ref, tnear_ref, tfar_ref, slices)


def local_kernel(x_ref, src_ref, links_ref, rate_ref, *refs, slices, keep):
    y_ref, behind_ref = refs[0], refs[-1]
    behind_ref[...] = jnp.zeros_like(behind_ref)

    def step(t, carry):
        load = lambda p, s, c: x_ref[t, 12 * p + 3 * s + c]
        acc = {}
        for direction in range(2):
            link = load_link(links_ref, slices, direction, t)
            ahead = map_half(moved(direction, 1), project(-1, direction, load))
            rebuild_into(acc, -1, direction, colour_mul(link, ahead, False))
            behind = colour_mul(link, project(1, direction, load), True)
            rebuild_into(acc, 1, direction, map_half(moved(direction, -1), behind))
        link = load_link(links_ref, slices, 3, t)
        inside = jnp.where(t == slices - 1, 0.0, 1.0)
        following = jnp.minimum(t + 1, slices - 1)
        ahead = project(-1, 3, lambda p, s, c: x_ref[following, 12 * p + 3 * s + c])
        ahead = map_half(lambda v: v * inside, ahead)
        rebuild_into(acc, -1, 3, colour_mul(link, ahead, False))
        rebuild_into(acc, 1, 3, load_half(lambda i: behind_ref[i]))
        up = colour_mul(link, project(1, 3, load), True)
        store_half(lambda i, v: behind_ref.__setitem__(i, v), up)
        rate = rate_ref[...]
        for (p, s, c), hop in acc.items():
            comp = 12 * p + 3 * s + c
            where = pl.ds(comp * slices + t, 8, stride=24 * slices)
            value = load(p, s, c)
            y_ref[t, comp] = value + rate * (src_ref[where, :] - (value - HOPPING * hop))
            if keep:
                refs[1][where, :] = value
        return carry

    lax.fori_loop(0, slices, step, 0)


def halo_kernel(
    y_ref, links_ref, rate_ref, znear_ref, zfar_ref, tnear_ref, tfar_ref, *refs, slices, final
):
    above_near = z_even()
    _, t_even = t_place()
    edge_ref = refs[-1]
    last = slices - 1
    near, far = (load_half(lambda i, ref=ref: ref[i]) for ref in (tnear_ref, tfar_ref))
    link = load_link(links_ref, slices, 3, last)
    above = colour_mul(link, choose(t_even, near, far), False)
    store_half(lambda i, v: edge_ref.__setitem__((0, i), v), above)
    store_half(lambda i, v: edge_ref.__setitem__((1, i), v), choose(t_even, far, near))

    def step(t, carry):
        acc = {}
        near, far = (load_half(lambda i, ref=ref: ref[t, i]) for ref in (znear_ref, zfar_ref))
        link = load_link(links_ref, slices, 2, t)
        rebuild_into(acc, -1, 2, colour_mul(link, choose(above_near, near, far), False))
        rebuild_into(acc, 1, 2, choose(above_near, far, near))
        top, bottom = (jnp.where(t == edge, 1.0, 0.0) for edge in (last, 0))
        rebuild_into(acc, -1, 3, map_half(lambda v: v * top, load_half(lambda i: edge_ref[0, i])))
        rebuild_into(acc, 1, 3, map_half(lambda v: v * bottom, load_half(lambda i: edge_ref[1, i])))
        rate = rate_ref[...] * HOPPING
        new = {}
        for (p, s, c), hop in acc.items():
            comp = 12 * p + 3 * s + c
            value = y_ref[t, comp] + rate * hop
            new[(p, s, c)] = value
            if final:
                refs[0][pl.ds(comp * slices + t, 8, stride=24 * slices), :] = value
            else:
                refs[0][t, comp] = value
        if not final:
            emit_halos(
                lambda p, s, c: new[(p, s, c)], links_ref, t, refs[1], refs[2], slices
            )
        return carry

    lax.fori_loop(0, slices, step, 0)
    if not final:
        emit_time_halos(refs[0], links_ref, refs[3], refs[4], slices)


def call(kernel, outs, ins, flops, hbm=(), smem=(), scratch=()):
    space = lambda i: pltpu.HBM if i in hbm else pltpu.SMEM if i in smem else pltpu.VMEM
    return pl.pallas_call(
        kernel,
        out_shape=outs,
        in_specs=[pl.BlockSpec(memory_space=space(i)) for i in range(ins)],
        out_specs=jax.tree.map(lambda _: pl.BlockSpec(memory_space=pltpu.VMEM), outs),
        scratch_shapes=list(scratch),
        compiler_params=pltpu.CompilerParams(vmem_limit_bytes=24 << 20),
        cost_estimate=pl.CostEstimate(
            flops=flops, bytes_accessed=3_000_000, transcendentals=0
        ),
    )


def exchange(send):
    znear, zfar, tnear, tfar = send
    nz, nt = lax.axis_size("src"), lax.axis_size(("lat", "sub"))
    near = lambda n: [(i, i ^ 1) for i in range(n)]
    far = lambda n: [(i, (i + 1 if i % 2 else i - 1) % n) for i in range(n)]

    return (
        lax.ppermute(znear, "src", near(nz)),
        lax.ppermute(zfar, "src", far(nz)),
        lax.ppermute(tnear, ("lat", "sub"), near(nt)),
        lax.ppermute(tfar, ("lat", "sub"), far(nt)),
    )


def shards(sources, eigvecs, eigvals, links, damping):
    count, comps, slices = sources.shape[:3]
    nev = eigvecs.shape[0]
    zdim = links.shape[3]
    devices = lax.axis_size(("src", "lat", "sub"))
    norm = math.sqrt(comps * slices * 128 * devices)
    f32 = jnp.float32

    src = sources.reshape(count * comps * slices, 128)
    eig = eigvecs.transpose(0, 2, 3, 1, 4).reshape(nev, slices, comps, 128)

    shape = lambda *dims: jax.ShapeDtypeStruct(dims, f32)
    lat, rest = lax.axis_size("lat"), lax.axis_size(("sub", "src"))
    links = links.reshape(4 * 18 * slices, zdim, 128)
    hbm = lambda x: pltpu.with_memory_space_constraint(x, pltpu.HBM)
    partial, eig, slot = call(
        functools.partial(correlation_kernel, nev=nev, slices=slices),
        (shape(lat, 8, 128), jax.ShapeDtypeStruct(eig.shape, eig.dtype), shape(8, 128)),
        2, 226_000_000, hbm=(0, 1),
        scratch=[
            pltpu.VMEM(src.shape, f32),
            pltpu.SemaphoreType.DMA((slices + 2,)),
        ],
    )(hbm(eig), hbm(src))
    partial = lax.all_to_all(partial, "lat", 0, 0, tiled=True)
    flat_links = call(
        slab_kernel, shape(4 * 18 * slices, 128), 1, 1000, hbm=(0,),
        scratch=[pltpu.SemaphoreType.DMA],
    )(hbm(links))
    partial = partial.sum(0) + slot * damping[0]
    partial = jnp.broadcast_to(partial[None], (rest, 8, 128))
    partial = lax.all_to_all(partial, ("sub", "src"), 0, 0, tiled=True)

    field = shape(slices, comps, 8, 128)
    halos = (shape(slices, 12, 8, 128),) * 2 + (shape(12, 8, 128),) * 2
    flat = shape(count * comps * slices, 128)
    x, rate, *send = call(
        functools.partial(guess_kernel, nev=nev, slices=slices, norm=norm),
        (field, shape(8, 128)) + halos, 4, 226_000_000,
    )(partial, eigvals.reshape(1, nev), eig, flat_links)

    guess = None
    for sweep in range(ITERS):
        final = sweep == ITERS - 1
        keep = sweep == 0
        got = exchange(send)
        y, *kept = call(
            functools.partial(local_kernel, slices=slices, keep=keep),
            (field,) + ((flat,) if keep else ()), 4, 10_000_000,
            scratch=[pltpu.VMEM((12, 8, 128), f32)],
        )(x, src, flat_links, rate)
        if keep:
            guess = kept[0]
        outs = flat if final else (field,) + halos
        res = call(
            functools.partial(halo_kernel, slices=slices, final=final),
            outs, 7, 5_000_000,
            scratch=[pltpu.VMEM((2, 12, 8, 128), f32)],
        )(y, flat_links, rate, *got)
        if final:
            x = res
        else:
            x, *send = res
    return (guess.reshape(sources.shape), x.reshape(sources.shape))


def solution(mesh):
    return jax.shard_map(
        shards,
        mesh=mesh,
        in_specs=(
            P(None, None, ("lat", "sub"), "src", None),
            P(None, None, ("lat", "sub"), "src", None),
            P(),
            P(None, None, ("lat", "sub"), None, None),
            P("src"),
        ),
        out_specs=(
            P(None, None, ("lat", "sub"), "src", None),
            P(None, None, ("lat", "sub"), "src", None),
        ),
        check_vma=False,
    )
```

```python
import functools
import math

import jax
import jax.numpy as jnp
from jax import lax
from jax.experimental import pallas as pl
from jax.experimental.pallas import tpu as pltpu
from jax.sharding import PartitionSpec as P

LX = 16
ITERS = 2
HOPPING = 0.12

BLOCKS = [
    {(0, 1): 1, (1, 0): 1},
    {(0, 1): 2, (1, 0): 0},
    {(0, 0): 1, (1, 1): 3},
    {(0, 0): 0, (1, 1): 0},
]


def times_power(power, re, im):
    return [
        ((1, re), (1, im)),
        ((-1, im), (1, re)),
        ((-1, re), (-1, im)),
        ((1, im), (-1, re)),
    ][power % 4]


def add_signed(base, sign, value):
    return base + value if sign > 0 else base - value


def project(sign, direction, load):
    half = []
    for row in range(2):
        col, power = next((c, p) for (r, c), p in BLOCKS[direction].items() if r == row)
        colours = []
        for colour in range(3):
            lower_re, lower_im = load(0, 2 + col, colour), load(1, 2 + col, colour)
            (sr, vr), (si, vi) = times_power(power, lower_re, lower_im)
            colours.append(
                (
                    add_signed(load(0, row, colour), sr * sign, vr),
                    add_signed(load(1, row, colour), si * sign, vi),
                )
            )
        half.append(colours)
    return half


def rebuild_into(acc, sign, direction, half):
    def put(key, sgn, value):
        if key in acc:
            acc[key] = add_signed(acc[key], sgn, value)
        else:
            acc[key] = value if sgn > 0 else -value

    for row in range(2):
        for colour in range(3):
            re, im = half[row][colour]
            put((0, row, colour), 1, re)
            put((1, row, colour), 1, im)
    for (row, col), power in BLOCKS[direction].items():
        for colour in range(3):
            re, im = half[row][colour]
            (sr, vr), (si, vi) = times_power(-power, re, im)
            put((0, 2 + col, colour), sr * sign, vr)
            put((1, 2 + col, colour), si * sign, vi)


def colour_mul(link, half, adjoint):
    out = []
    for spin in range(2):
        rows = []
        for row in range(3):
            re = im = None
            for col in range(3):
                lr, li = link[(col, row)] if adjoint else link[(row, col)]
                hr, hi = half[spin][col]
                if adjoint:
                    tr, ti = lr * hr + li * hi, lr * hi - li * hr
                else:
                    tr, ti = lr * hr - li * hi, lr * hi + li * hr
                re = tr if re is None else re + tr
                im = ti if im is None else im + ti
            rows.append((re, im))
        out.append(rows)
    return out


def map_half(fn, half):
    return [[(fn(re), fn(im)) for re, im in rows] for rows in half]


def load_half(load):
    return [[(load(3 * s + c), load(6 + 3 * s + c)) for c in range(3)] for s in range(2)]


def store_half(store, half):
    for s in range(2):
        for c in range(3):
            store(3 * s + c, half[s][c][0])
            store(6 + 3 * s + c, half[s][c][1])


def load_link(links_ref, slices, direction, t):
    def one(comp):
        row = (direction * 18 + comp) * slices + t
        return jnp.broadcast_to(links_ref[pl.ds(row, 1), :], (8, 128))

    return {(a, c): (one(3 * a + c), one(9 + 3 * a + c)) for a in range(3) for c in range(3)}


def moved(direction, step):
    def fn(v):
        if direction == 1:
            return pltpu.roll(v, (-step * LX) % 128, 1)
        column = lax.rem(lax.broadcasted_iota(jnp.int32, v.shape, 1), LX)
        border = LX - 1 if step > 0 else 0
        inside = pltpu.roll(v, (-step) % 128, 1)
        wrapped = pltpu.roll(v, (step * (LX - 1)) % 128, 1)
        return jnp.where(column == border, wrapped, inside)

    return fn


def correlation_kernel(
    eig_hbm, src_hbm, out_ref, eig_ref, slot_ref, src_ref, sems, *, nev, slices
):
    comps = 24
    sources = 8
    rows = sources * comps * slices // 2
    src_copies = [
        pltpu.make_async_copy(
            src_hbm.at[pl.ds(i * rows, rows)], src_ref.at[pl.ds(i * rows, rows)], sems.at[slices + i]
        )
        for i in range(2)
    ]
    eig_copies = [
        pltpu.make_async_copy(eig_hbm.at[:, t], eig_ref.at[:, t], sems.at[t]) for t in range(slices)
    ]
    for copy in src_copies + eig_copies:
        copy.start()
    for copy in src_copies:
        copy.wait()
    full = jnp.zeros((sources * comps, nev * comps), jnp.float32)
    for t in range(0, slices, 2):
        lhs = [
            src_ref[pl.ds(u, sources * comps, stride=slices), :].astype(jnp.bfloat16)
            for u in (t, t + 1)
        ]
        eig_copies[t].wait()
        eig_copies[t + 1].wait()
        rhs = [eig_ref[:, u].reshape(nev * comps, 128) for u in (t, t + 1)]
        full = full + lax.dot_general(
            jnp.concatenate(lhs, axis=1), jnp.concatenate(rhs, axis=1),
            (((1,), (1,)), ((), ())), preferred_element_type=jnp.float32,
        )
    row = lax.rem(lax.broadcasted_iota(jnp.int32, (sources * comps, 1), 0), comps)
    col = lax.rem(lax.broadcasted_iota(jnp.int32, (1, nev * comps), 1), comps)
    gap = row - col
    straight = jnp.where(gap == 0, full, 0.0)
    crossed = jnp.where(gap == 12, full, 0.0) - jnp.where(gap == -12, full, 0.0)
    straight = straight.reshape(sources, comps, nev * comps).sum(1)
    crossed = crossed.reshape(sources, comps, nev * comps).sum(1)
    first = lax.broadcasted_iota(jnp.int32, (nev * comps, 128), 0)
    lane = lax.broadcasted_iota(jnp.int32, (nev * comps, 128), 1)

    def gather(which):
        start = (lane - which * nev) * comps
        return jnp.where((first >= start) & (first < start + comps), 1.0, 0.0)

    dot = functools.partial(
        jnp.dot, precision=lax.Precision.HIGHEST, preferred_element_type=jnp.float32
    )
    total = dot(straight, gather(0)) + dot(crossed, gather(1))
    out_ref[...] = jnp.broadcast_to(total[None], out_ref.shape)
    at_row = lax.broadcasted_iota(jnp.int32, (8, 128), 0) == lax.axis_index("src")
    at_lane = lax.broadcasted_iota(jnp.int32, (8, 128), 1) == 2 * nev
    holder = jnp.where(lax.axis_index("sub") == 0, 1.0, 0.0)
    slot_ref[...] = jnp.where(at_row & at_lane, holder, 0.0)


def fringe_kernel(eig_ref, links_hbm, links_ref, near_ref, far_ref, sem, *, nev, slices):
    copy = pltpu.make_async_copy(links_hbm.at[:, lax.axis_index("src")], links_ref, sem)
    copy.start()
    place, even = t_place()
    extent = lax.axis_size(("lat", "sub"))
    half = nev * 12
    row = lax.broadcasted_iota(jnp.int32, (half, 1), 0)
    part = lax.rem(row, 12)
    upper = 2 * (row - part) + part + jnp.where(part >= 6, 6, 0)
    col = lax.broadcasted_iota(jnp.int32, (1, nev * 24), 1)
    gap = col - upper

    def edge(sign, t, flip):
        pick = jnp.where(gap == 0, 1.0, jnp.where(gap == 6, float(sign), 0.0)).astype(jnp.bfloat16)
        modes = eig_ref[:, t].reshape(nev * 24, 128)
        value = jnp.dot(pick, modes, preferred_element_type=jnp.float32)
        return value * jnp.where(flip, -1.0, 1.0)

    up = edge(1, slices - 1, place == extent - 1)
    down = edge(-1, 0, place == 0)
    near_ref[0:half, :] = jnp.where(even, up, down)
    far_ref[0:half, :] = jnp.where(even, down, up)
    copy.wait()
    for comp in range(18):
        link = links_ref[pl.ds((3 * 18 + comp) * slices + slices - 1, 1), :]
        near_ref[half + comp : half + comp + 1, :] = link
        far_ref[half + comp : half + comp + 1, :] = link
    rest = near_ref.shape[0] - half - 18
    near_ref[half + 18 :, :] = jnp.zeros((rest, 128), jnp.float32)
    far_ref[half + 18 :, :] = jnp.zeros((rest, 128), jnp.float32)


def choose(flag, half_true, half_false):
    return [
        [
            tuple(jnp.where(flag, a, b) for a, b in zip(half_true[s][c], half_false[s][c]))
            for c in range(3)
        ]
        for s in range(2)
    ]


def z_even():
    return lax.rem(lax.axis_index("src"), 2) == 0


def t_place():
    place = lax.axis_index(("lat", "sub"))
    return place, lax.rem(place, 2) == 0


def emit_halos(load, links_ref, t, near_ref, far_ref, slices):
    even = z_even()
    up = project(1, 2, load)
    up = colour_mul(load_link(links_ref, slices, 2, t), up, True)
    down = project(-1, 2, load)
    store_half(lambda i, v: near_ref.__setitem__((t, i), v), choose(even, up, down))
    store_half(lambda i, v: far_ref.__setitem__((t, i), v), choose(even, down, up))


def emit_time_halos(x_ref, links_ref, near_ref, far_ref, slices):
    place, even = t_place()
    extent = lax.axis_size(("lat", "sub"))
    up_sign = jnp.where(place == extent - 1, -1.0, 1.0)
    down_sign = jnp.where(place == 0, -1.0, 1.0)
    last = slices - 1
    up = project(1, 3, lambda p, s, c: x_ref[last, 12 * p + 3 * s + c])
    up = colour_mul(load_link(links_ref, slices, 3, last), up, True)
    up = map_half(lambda v: v * up_sign, up)
    down = project(-1, 3, lambda p, s, c: x_ref[0, 12 * p + 3 * s + c])
    down = map_half(lambda v: v * down_sign, down)
    store_half(lambda i, v: near_ref.__setitem__(i, v), choose(even, up, down))
    store_half(lambda i, v: far_ref.__setitem__(i, v), choose(even, down, up))


def guess_kernel(
    part_ref, ev_ref, eig_ref, links_ref, near_ref, far_ref,
    x_ref, rate_ref, znear_ref, zfar_ref, tbelow_ref, tabove_ref,
    *, nev, slices, norm,
):
    comps = 24
    total = part_ref[0]
    for i in range(1, part_ref.shape[0]):
        total = total + part_ref[i]
    ev = ev_ref[...]
    w_re = ((total[:, :nev] / norm) / ev).astype(jnp.bfloat16)
    w_im = ((total[:, nev : 2 * nev] / norm) / ev).astype(jnp.bfloat16)
    rate_ref[...] = jnp.broadcast_to(total[:, 2 * nev : 2 * nev + 1], (8, 128))

    def mixing(width, offset):
        row = lax.broadcasted_iota(jnp.int32, (nev, nev * width), 0) * width
        col = lax.broadcasted_iota(jnp.int32, (nev, nev * width), 1)
        spread = jnp.where((col >= row) & (col < row + width), 1.0, 0.0).astype(jnp.bfloat16)
        re = jnp.dot(w_re, spread, preferred_element_type=jnp.float32)
        im = jnp.dot(w_im, spread, preferred_element_type=jnp.float32)
        comp = lax.rem(lax.broadcasted_iota(jnp.int32, (8, nev * width), 1), width)
        blocks = []
        for c in range(width):
            other, turned = (c + offset, -im) if c < offset else (c - offset, im)
            blocks.append(jnp.where(comp == c, re, jnp.where(comp == other, turned, 0.0)))
        return jnp.concatenate(blocks, axis=0)

    mix = mixing(comps, 12).astype(jnp.bfloat16)
    for t in range(slices):
        res = jnp.dot(
            mix, eig_ref[:, t].reshape(nev * comps, 128), preferred_element_type=jnp.float32
        )
        x_ref[t] = res.reshape(comps, 8, 128)

    def step(t, carry):
        emit_halos(
            lambda p, s, c: x_ref[t, 12 * p + 3 * s + c],
            links_ref, t, znear_ref, zfar_ref, slices,
        )
        return carry

    lax.fori_loop(0, slices, step, 0)
    half = nev * 12
    mix = mixing(12, 6)
    near, far = (
        jnp.dot(
            mix, ref[0:half, :], precision=lax.Precision.HIGHEST, preferred_element_type=jnp.float32
        ).reshape(12, 8, 128)
        for ref in (near_ref, far_ref)
    )
    near, far = (load_half(lambda i, v=v: v[i]) for v in (near, far))
    _, even = t_place()

    def link_of(comp):
        rows = [ref[half + comp : half + comp + 1, :] for ref in (far_ref, near_ref)]
        return jnp.broadcast_to(jnp.where(even, *rows), (8, 128))

    link = {
        (a, c): (link_of(3 * a + c), link_of(9 + 3 * a + c)) for a in range(3) for c in range(3)
    }
    below = colour_mul(link, choose(even, far, near), True)
    store_half(lambda i, v: tbelow_ref.__setitem__(i, v), below)
    store_half(lambda i, v: tabove_ref.__setitem__(i, v), choose(even, near, far))


def local_kernel(x_ref, src_ref, links_ref, rate_ref, *refs, slices, keep):
    y_ref, behind_ref = refs[0], refs[-1]
    behind_ref[...] = jnp.zeros_like(behind_ref)

    def step(t, carry):
        load = lambda p, s, c: x_ref[t, 12 * p + 3 * s + c]
        acc = {}
        for direction in range(2):
            link = load_link(links_ref, slices, direction, t)
            ahead = map_half(moved(direction, 1), project(-1, direction, load))
            rebuild_into(acc, -1, direction, colour_mul(link, ahead, False))
            behind = colour_mul(link, project(1, direction, load), True)
            rebuild_into(acc, 1, direction, map_half(moved(direction, -1), behind))
        link = load_link(links_ref, slices, 3, t)
        inside = jnp.where(t == slices - 1, 0.0, 1.0)
        following = jnp.minimum(t + 1, slices - 1)
        ahead = project(-1, 3, lambda p, s, c: x_ref[following, 12 * p + 3 * s + c])
        ahead = map_half(lambda v: v * inside, ahead)
        rebuild_into(acc, -1, 3, colour_mul(link, ahead, False))
        rebuild_into(acc, 1, 3, load_half(lambda i: behind_ref[i]))
        up = colour_mul(link, project(1, 3, load), True)
        store_half(lambda i, v: behind_ref.__setitem__(i, v), up)
        rate = rate_ref[...]
        for (p, s, c), hop in acc.items():
            comp = 12 * p + 3 * s + c
            where = pl.ds(comp * slices + t, 8, stride=24 * slices)
            value = load(p, s, c)
            y_ref[t, comp] = value + rate * (src_ref[where, :] - (value - HOPPING * hop))
            if keep:
                refs[1][where, :] = value
        return carry

    lax.fori_loop(0, slices, step, 0)


def halo_kernel(
    y_ref, links_ref, rate_ref, znear_ref, zfar_ref, tnear_ref, tfar_ref, *refs, slices, final, sorted_t
):
    above_near = z_even()
    _, t_even = t_place()
    edge_ref = refs[-1]
    last = slices - 1
    near, far = (load_half(lambda i, ref=ref: ref[i]) for ref in (tnear_ref, tfar_ref))
    link = load_link(links_ref, slices, 3, last)
    below, above = (near, far) if sorted_t else (choose(t_even, far, near), choose(t_even, near, far))
    store_half(lambda i, v: edge_ref.__setitem__((0, i), v), colour_mul(link, above, False))
    store_half(lambda i, v: edge_ref.__setitem__((1, i), v), below)

    def step(t, carry):
        acc = {}
        near, far = (load_half(lambda i, ref=ref: ref[t, i]) for ref in (znear_ref, zfar_ref))
        link = load_link(links_ref, slices, 2, t)
        rebuild_into(acc, -1, 2, colour_mul(link, choose(above_near, near, far), False))
        rebuild_into(acc, 1, 2, choose(above_near, far, near))
        top, bottom = (jnp.where(t == edge, 1.0, 0.0) for edge in (last, 0))
        rebuild_into(acc, -1, 3, map_half(lambda v: v * top, load_half(lambda i: edge_ref[0, i])))
        rebuild_into(acc, 1, 3, map_half(lambda v: v * bottom, load_half(lambda i: edge_ref[1, i])))
        rate = rate_ref[...] * HOPPING
        new = {}
        for (p, s, c), hop in acc.items():
            comp = 12 * p + 3 * s + c
            value = y_ref[t, comp] + rate * hop
            new[(p, s, c)] = value
            if final:
                refs[0][pl.ds(comp * slices + t, 8, stride=24 * slices), :] = value
            else:
                refs[0][t, comp] = value
        if not final:
            emit_halos(
                lambda p, s, c: new[(p, s, c)], links_ref, t, refs[1], refs[2], slices
            )
        return carry

    lax.fori_loop(0, slices, step, 0)
    if not final:
        emit_time_halos(refs[0], links_ref, refs[3], refs[4], slices)


def call(kernel, outs, ins, flops, hbm=(), smem=(), scratch=()):
    space = lambda i: pltpu.HBM if i in hbm else pltpu.SMEM if i in smem else pltpu.VMEM
    return pl.pallas_call(
        kernel,
        out_shape=outs,
        in_specs=[pl.BlockSpec(memory_space=space(i)) for i in range(ins)],
        out_specs=jax.tree.map(lambda _: pl.BlockSpec(memory_space=pltpu.VMEM), outs),
        scratch_shapes=list(scratch),
        compiler_params=pltpu.CompilerParams(vmem_limit_bytes=24 << 20),
        cost_estimate=pl.CostEstimate(
            flops=flops, bytes_accessed=3_000_000, transcendentals=0
        ),
    )


def swap(x, axis, far):
    n = lax.axis_size(axis)
    partner = lambda i: (i + 1 if i % 2 else i - 1) % n if far else i ^ 1
    return lax.ppermute(x, axis, [(i, partner(i)) for i in range(n)])


def shards(sources, eigvecs, eigvals, links, damping):
    count, comps, slices = sources.shape[:3]
    nev = eigvecs.shape[0]
    zdim = links.shape[3]
    devices = lax.axis_size(("src", "lat", "sub"))
    norm = math.sqrt(comps * slices * 128 * devices)
    f32 = jnp.float32

    src = sources.reshape(count * comps * slices, 128)
    eig = eigvecs.transpose(0, 2, 3, 1, 4).reshape(nev, slices, comps, 128)

    shape = lambda *dims: jax.ShapeDtypeStruct(dims, f32)
    lat, rest = lax.axis_size("lat"), lax.axis_size(("sub", "src"))
    links = links.reshape(4 * 18 * slices, zdim, 128)
    hbm = lambda x: pltpu.with_memory_space_constraint(x, pltpu.HBM)
    partial, eig, slot = call(
        functools.partial(correlation_kernel, nev=nev, slices=slices),
        (shape(lat, 8, 128), jax.ShapeDtypeStruct(eig.shape, eig.dtype), shape(8, 128)),
        2, 226_000_000, hbm=(0, 1),
        scratch=[
            pltpu.VMEM(src.shape, f32),
            pltpu.SemaphoreType.DMA((slices + 2,)),
        ],
    )(hbm(eig), hbm(src))
    partial = lax.all_to_all(partial, "lat", 0, 0, tiled=True)
    fringe = shape(nev * 12 + 24, 128)
    flat_links, near, far = call(
        functools.partial(fringe_kernel, nev=nev, slices=slices),
        (shape(4 * 18 * slices, 128), fringe, fringe), 2, 1000, hbm=(1,),
        scratch=[pltpu.SemaphoreType.DMA],
    )(eig, hbm(links))
    time = ("lat", "sub")
    far = swap(far, time, True)
    near = swap(near, time, False)
    partial = partial.sum(0) + slot * damping[0]
    partial = jnp.broadcast_to(partial[None], (rest, 8, 128))
    partial = lax.all_to_all(partial, ("sub", "src"), 0, 0, tiled=True)

    field = shape(slices, comps, 8, 128)
    halos = (shape(slices, 12, 8, 128),) * 2 + (shape(12, 8, 128),) * 2
    flat = shape(count * comps * slices, 128)
    x, rate, *send = call(
        functools.partial(guess_kernel, nev=nev, slices=slices, norm=norm),
        (field, shape(8, 128)) + halos, 6, 226_000_000,
    )(partial, eigvals.reshape(1, nev), eig, flat_links, near, far)

    guess = None
    for sweep in range(ITERS):
        final = sweep == ITERS - 1
        keep = sweep == 0
        got = [swap(send[0], "src", False), swap(send[1], "src", True)]
        if sweep == 0:
            got += send[2:]
        else:
            got += [swap(send[2], time, False), swap(send[3], time, True)]
        y, *kept = call(
            functools.partial(local_kernel, slices=slices, keep=keep),
            (field,) + ((flat,) if keep else ()), 4, 10_000_000,
            scratch=[pltpu.VMEM((12, 8, 128), f32)],
        )(x, src, flat_links, rate)
        if keep:
            guess = kept[0]
        outs = flat if final else (field,) + halos
        res = call(
            functools.partial(halo_kernel, slices=slices, final=final, sorted_t=sweep == 0),
            outs, 7, 5_000_000,
            scratch=[pltpu.VMEM((2, 12, 8, 128), f32)],
        )(y, flat_links, rate, *got)
        if final:
            x = res
        else:
            x, *send = res
    return (guess.reshape(sources.shape), x.reshape(sources.shape))


def solution(mesh):
    return jax.shard_map(
        shards,
        mesh=mesh,
        in_specs=(
            P(None, None, ("lat", "sub"), "src", None),
            P(None, None, ("lat", "sub"), "src", None),
            P(),
            P(None, None, ("lat", "sub"), None, None),
            P("src"),
        ),
        out_specs=(
            P(None, None, ("lat", "sub"), "src", None),
            P(None, None, ("lat", "sub"), "src", None),
        ),
        check_vma=False,
    )
```

```python
import functools
import math

import jax
import jax.numpy as jnp
from jax import lax
from jax.experimental import pallas as pl
from jax.experimental.pallas import tpu as pltpu
from jax.sharding import PartitionSpec as P

LX = 16
ITERS = 2
HOPPING = 0.12

BLOCKS = [
    {(0, 1): 1, (1, 0): 1},
    {(0, 1): 2, (1, 0): 0},
    {(0, 0): 1, (1, 1): 3},
    {(0, 0): 0, (1, 1): 0},
]


def times_power(power, re, im):
    return [
        ((1, re), (1, im)),
        ((-1, im), (1, re)),
        ((-1, re), (-1, im)),
        ((1, im), (-1, re)),
    ][power % 4]


def add_signed(base, sign, value):
    return base + value if sign > 0 else base - value


def project(sign, direction, load):
    half = []
    for row in range(2):
        col, power = next((c, p) for (r, c), p in BLOCKS[direction].items() if r == row)
        colours = []
        for colour in range(3):
            lower_re, lower_im = load(0, 2 + col, colour), load(1, 2 + col, colour)
            (sr, vr), (si, vi) = times_power(power, lower_re, lower_im)
            colours.append(
                (
                    add_signed(load(0, row, colour), sr * sign, vr),
                    add_signed(load(1, row, colour), si * sign, vi),
                )
            )
        half.append(colours)
    return half


def rebuild_into(acc, sign, direction, half):
    def put(key, sgn, value):
        if key in acc:
            acc[key] = add_signed(acc[key], sgn, value)
        else:
            acc[key] = value if sgn > 0 else -value

    for row in range(2):
        for colour in range(3):
            re, im = half[row][colour]
            put((0, row, colour), 1, re)
            put((1, row, colour), 1, im)
    for (row, col), power in BLOCKS[direction].items():
        for colour in range(3):
            re, im = half[row][colour]
            (sr, vr), (si, vi) = times_power(-power, re, im)
            put((0, 2 + col, colour), sr * sign, vr)
            put((1, 2 + col, colour), si * sign, vi)


def colour_mul(link, half, adjoint):
    out = []
    for spin in range(2):
        rows = []
        for row in range(3):
            re = im = None
            for col in range(3):
                lr, li = link[(col, row)] if adjoint else link[(row, col)]
                hr, hi = half[spin][col]
                if adjoint:
                    tr, ti = lr * hr + li * hi, lr * hi - li * hr
                else:
                    tr, ti = lr * hr - li * hi, lr * hi + li * hr
                re = tr if re is None else re + tr
                im = ti if im is None else im + ti
            rows.append((re, im))
        out.append(rows)
    return out


def map_half(fn, half):
    return [[(fn(re), fn(im)) for re, im in rows] for rows in half]


def load_half(load):
    return [[(load(3 * s + c), load(6 + 3 * s + c)) for c in range(3)] for s in range(2)]


def store_half(store, half):
    for s in range(2):
        for c in range(3):
            store(3 * s + c, half[s][c][0])
            store(6 + 3 * s + c, half[s][c][1])


def load_link(links_ref, slices, direction, t):
    def one(comp):
        row = (direction * 18 + comp) * slices + t
        return jnp.broadcast_to(links_ref[pl.ds(row, 1), :], (8, 128))

    return {(a, c): (one(3 * a + c), one(9 + 3 * a + c)) for a in range(3) for c in range(3)}


def moved(direction, step):
    def fn(v):
        if direction == 1:
            return pltpu.roll(v, (-step * LX) % 128, 1)
        column = lax.rem(lax.broadcasted_iota(jnp.int32, v.shape, 1), LX)
        border = LX - 1 if step > 0 else 0
        inside = pltpu.roll(v, (-step) % 128, 1)
        wrapped = pltpu.roll(v, (step * (LX - 1)) % 128, 1)
        return jnp.where(column == border, wrapped, inside)

    return fn


def correlation_kernel(
    eig_hbm, src_hbm, damp_ref, out_ref, eig_ref, src_ref, sems, *, nev, slices
):
    comps = 24
    sources = 8
    rows = sources * comps * slices // 2
    src_copies = [
        pltpu.make_async_copy(
            src_hbm.at[pl.ds(i * rows, rows)], src_ref.at[pl.ds(i * rows, rows)], sems.at[slices + i]
        )
        for i in range(2)
    ]
    eig_copies = [
        pltpu.make_async_copy(eig_hbm.at[:, t], eig_ref.at[:, t], sems.at[t]) for t in range(slices)
    ]
    for copy in src_copies + eig_copies:
        copy.start()
    for copy in src_copies:
        copy.wait()
    full = jnp.zeros((sources * comps, nev * comps), jnp.float32)
    for t in range(0, slices, 2):
        lhs = [
            src_ref[pl.ds(u, sources * comps, stride=slices), :].astype(jnp.bfloat16)
            for u in (t, t + 1)
        ]
        eig_copies[t].wait()
        eig_copies[t + 1].wait()
        rhs = [eig_ref[:, u].reshape(nev * comps, 128) for u in (t, t + 1)]
        full = full + lax.dot_general(
            jnp.concatenate(lhs, axis=1), jnp.concatenate(rhs, axis=1),
            (((1,), (1,)), ((), ())), preferred_element_type=jnp.float32,
        )
    row = lax.rem(lax.broadcasted_iota(jnp.int32, (sources * comps, 1), 0), comps)
    col = lax.rem(lax.broadcasted_iota(jnp.int32, (1, nev * comps), 1), comps)
    gap = row - col
    straight = jnp.where(gap == 0, full, 0.0)
    crossed = jnp.where(gap == 12, full, 0.0) - jnp.where(gap == -12, full, 0.0)
    straight = straight.reshape(sources, comps, nev * comps).sum(1)
    crossed = crossed.reshape(sources, comps, nev * comps).sum(1)
    first = lax.broadcasted_iota(jnp.int32, (nev * comps, 128), 0)
    lane = lax.broadcasted_iota(jnp.int32, (nev * comps, 128), 1)

    def gather(which):
        start = (lane - which * nev) * comps
        return jnp.where((first >= start) & (first < start + comps), 1.0, 0.0)

    dot = functools.partial(
        jnp.dot, precision=lax.Precision.HIGHEST, preferred_element_type=jnp.float32
    )
    total = dot(straight, gather(0)) + dot(crossed, gather(1))
    holder = (lax.axis_index("lat") == 0) & (lax.axis_index("sub") == 0)
    value = jnp.where(holder, damp_ref[0], 0.0)
    at_row = lax.broadcasted_iota(jnp.int32, (8, 128), 0) == lax.axis_index("src")
    at_lane = lax.broadcasted_iota(jnp.int32, (8, 128), 1) == 2 * nev
    total = total + jnp.where(at_row & at_lane, value, 0.0)
    out_ref[...] = jnp.broadcast_to(total[None], out_ref.shape)


def choose(flag, half_true, half_false):
    return [
        [
            tuple(jnp.where(flag, a, b) for a, b in zip(half_true[s][c], half_false[s][c]))
            for c in range(3)
        ]
        for s in range(2)
    ]


def z_even():
    return lax.rem(lax.axis_index("src"), 2) == 0


def t_place():
    place = lax.axis_index(("lat", "sub"))
    return place, lax.rem(place, 2) == 0


def emit_halos(load, links_ref, t, near_ref, far_ref, slices):
    even = z_even()
    up = project(1, 2, load)
    up = colour_mul(load_link(links_ref, slices, 2, t), up, True)
    down = project(-1, 2, load)
    store_half(lambda i, v: near_ref.__setitem__((t, i), v), choose(even, up, down))
    store_half(lambda i, v: far_ref.__setitem__((t, i), v), choose(even, down, up))


def emit_time_halos(load_last, load_first, links_ref, near_ref, far_ref, slices):
    place, even = t_place()
    extent = lax.axis_size(("lat", "sub"))
    up_sign = jnp.where(place == extent - 1, -1.0, 1.0)
    down_sign = jnp.where(place == 0, -1.0, 1.0)
    last = slices - 1
    up = project(1, 3, load_last)
    up = colour_mul(load_link(links_ref, slices, 3, last), up, True)
    up = map_half(lambda v: v * up_sign, up)
    down = project(-1, 3, load_first)
    down = map_half(lambda v: v * down_sign, down)
    store_half(lambda i, v: near_ref.__setitem__(i, v), choose(even, up, down))
    store_half(lambda i, v: far_ref.__setitem__(i, v), choose(even, down, up))


def guess_kernel(
    part_ref, ev_ref, eig_ref, links_hbm,
    x_ref, links_ref, rate_ref, guess_ref, znear_ref, zfar_ref, tnear_ref, tfar_ref, sems,
    *, nev, slices, norm,
):
    comps = 24
    copies = []
    for i, first in enumerate((2, 0)):
        rows = pl.ds(first * 18 * slices, 2 * 18 * slices)
        copies.append(
            pltpu.make_async_copy(
                links_hbm.at[rows, lax.axis_index("src")], links_ref.at[rows], sems.at[i]
            )
        )
        copies[-1].start()
    total = part_ref[0]
    for i in range(1, part_ref.shape[0]):
        total = total + part_ref[i]
    ev = ev_ref[...]
    w_re = ((total[:, :nev] / norm) / ev).astype(jnp.bfloat16)
    w_im = ((total[:, nev : 2 * nev] / norm) / ev).astype(jnp.bfloat16)
    rate_ref[...] = jnp.broadcast_to(total[:, 2 * nev : 2 * nev + 1], (8, 128))
    row = lax.broadcasted_iota(jnp.int32, (nev, nev * comps), 0) * comps
    col = lax.broadcasted_iota(jnp.int32, (nev, nev * comps), 1)
    spread = jnp.where((col >= row) & (col < row + comps), 1.0, 0.0).astype(jnp.bfloat16)
    w_re = jnp.dot(w_re, spread, preferred_element_type=jnp.float32)
    w_im = jnp.dot(w_im, spread, preferred_element_type=jnp.float32)
    comp = lax.rem(lax.broadcasted_iota(jnp.int32, (8, nev * comps), 1), comps)
    blocks = []
    for c in range(comps):
        other, turned = (c + 12, -w_im) if c < 12 else (c - 12, w_im)
        blocks.append(jnp.where(comp == c, w_re, jnp.where(comp == other, turned, 0.0)))
    mix = jnp.concatenate(blocks, axis=0).astype(jnp.bfloat16)
    for t in range(slices):
        res = jnp.dot(
            mix, eig_ref[:, t].reshape(nev * comps, 128), preferred_element_type=jnp.float32
        )
        x_ref[t] = res.reshape(comps, 8, 128)
    copies[0].wait()

    def step(t, carry):
        for c in range(comps):
            guess_ref[pl.ds(c * slices + t, 8, stride=comps * slices), :] = x_ref[t, c]
        emit_halos(
            lambda p, s, c: x_ref[t, 12 * p + 3 * s + c],
            links_ref, t, znear_ref, zfar_ref, slices,
        )
        return carry

    lax.fori_loop(0, slices, step, 0)
    load = lambda t: lambda p, s, c: x_ref[t, 12 * p + 3 * s + c]
    emit_time_halos(load(slices - 1), load(0), links_ref, tnear_ref, tfar_ref, slices)
    copies[1].wait()


def local_kernel(x_ref, src_ref, links_ref, rate_ref, y_ref, behind_ref, *, slices):
    behind_ref[...] = jnp.zeros_like(behind_ref)

    def step(t, carry):
        load = lambda p, s, c: x_ref[t, 12 * p + 3 * s + c]
        acc = {}
        for direction in range(2):
            link = load_link(links_ref, slices, direction, t)
            ahead = map_half(moved(direction, 1), project(-1, direction, load))
            rebuild_into(acc, -1, direction, colour_mul(link, ahead, False))
            behind = colour_mul(link, project(1, direction, load), True)
            rebuild_into(acc, 1, direction, map_half(moved(direction, -1), behind))
        link = load_link(links_ref, slices, 3, t)
        inside = jnp.where(t == slices - 1, 0.0, 1.0)
        following = jnp.minimum(t + 1, slices - 1)
        ahead = project(-1, 3, lambda p, s, c: x_ref[following, 12 * p + 3 * s + c])
        ahead = map_half(lambda v: v * inside, ahead)
        rebuild_into(acc, -1, 3, colour_mul(link, ahead, False))
        rebuild_into(acc, 1, 3, load_half(lambda i: behind_ref[i]))
        up = colour_mul(link, project(1, 3, load), True)
        store_half(lambda i, v: behind_ref.__setitem__(i, v), up)
        rate = rate_ref[...]
        for (p, s, c), hop in acc.items():
            comp = 12 * p + 3 * s + c
            where = pl.ds(comp * slices + t, 8, stride=24 * slices)
            value = load(p, s, c)
            y_ref[t, comp] = value + rate * (src_ref[where, :] - (value - HOPPING * hop))
        return carry

    lax.fori_loop(0, slices, step, 0)


def z_hops(links_ref, znear_ref, zfar_ref, t, slices):
    above_near = z_even()
    acc = {}
    near, far = (load_half(lambda i, ref=ref: ref[t, i]) for ref in (znear_ref, zfar_ref))
    link = load_link(links_ref, slices, 2, t)
    rebuild_into(acc, -1, 2, colour_mul(link, choose(above_near, near, far), False))
    rebuild_into(acc, 1, 2, choose(above_near, far, near))
    return acc


def edge_kernel(y_ref, links_ref, rate_ref, znear_ref, zfar_ref, tnear_ref, tfar_ref, *, slices):
    rate = rate_ref[...] * HOPPING

    def load(t):
        hops = z_hops(links_ref, znear_ref, zfar_ref, t, slices)
        return lambda p, s, c: y_ref[t, 12 * p + 3 * s + c] + rate * hops[(p, s, c)]

    emit_time_halos(load(slices - 1), load(0), links_ref, tnear_ref, tfar_ref, slices)


def halo_kernel(
    y_ref, links_ref, rate_ref, znear_ref, zfar_ref, tnear_ref, tfar_ref, *refs, slices, final
):
    _, t_even = t_place()
    edge_ref = refs[-1]
    last = slices - 1
    near, far = (load_half(lambda i, ref=ref: ref[i]) for ref in (tnear_ref, tfar_ref))
    link = load_link(links_ref, slices, 3, last)
    above = colour_mul(link, choose(t_even, near, far), False)
    store_half(lambda i, v: edge_ref.__setitem__((0, i), v), above)
    store_half(lambda i, v: edge_ref.__setitem__((1, i), v), choose(t_even, far, near))

    def step(t, carry):
        acc = z_hops(links_ref, znear_ref, zfar_ref, t, slices)
        top, bottom = (jnp.where(t == edge, 1.0, 0.0) for edge in (last, 0))
        rebuild_into(acc, -1, 3, map_half(lambda v: v * top, load_half(lambda i: edge_ref[0, i])))
        rebuild_into(acc, 1, 3, map_half(lambda v: v * bottom, load_half(lambda i: edge_ref[1, i])))
        rate = rate_ref[...] * HOPPING
        new = {}
        for (p, s, c), hop in acc.items():
            comp = 12 * p + 3 * s + c
            value = y_ref[t, comp] + rate * hop
            new[(p, s, c)] = value
            if final:
                refs[0][pl.ds(comp * slices + t, 8, stride=24 * slices), :] = value
            else:
                refs[0][t, comp] = value
        if not final:
            emit_halos(
                lambda p, s, c: new[(p, s, c)], links_ref, t, refs[1], refs[2], slices
            )
        return carry

    lax.fori_loop(0, slices, step, 0)


def call(kernel, outs, ins, flops, hbm=(), smem=(), scratch=()):
    space = lambda i: pltpu.HBM if i in hbm else pltpu.SMEM if i in smem else pltpu.VMEM
    return pl.pallas_call(
        kernel,
        out_shape=outs,
        in_specs=[pl.BlockSpec(memory_space=space(i)) for i in range(ins)],
        out_specs=jax.tree.map(lambda _: pl.BlockSpec(memory_space=pltpu.VMEM), outs),
        scratch_shapes=list(scratch),
        compiler_params=pltpu.CompilerParams(vmem_limit_bytes=24 << 20),
        cost_estimate=pl.CostEstimate(
            flops=flops, bytes_accessed=3_000_000, transcendentals=0
        ),
    )


def swap(x, axis, far):
    n = lax.axis_size(axis)
    partner = lambda i: (i + 1 if i % 2 else i - 1) % n if far else i ^ 1
    return lax.ppermute(x, axis, [(i, partner(i)) for i in range(n)])


def shards(sources, eigvecs, eigvals, links, damping):
    count, comps, slices = sources.shape[:3]
    nev = eigvecs.shape[0]
    zdim = links.shape[3]
    devices = lax.axis_size(("src", "lat", "sub"))
    norm = math.sqrt(comps * slices * 128 * devices)
    f32 = jnp.float32

    src = sources.reshape(count * comps * slices, 128)
    eig = eigvecs.transpose(0, 2, 3, 1, 4).reshape(nev, slices, comps, 128)

    shape = lambda *dims: jax.ShapeDtypeStruct(dims, f32)
    lat, rest = lax.axis_size("lat"), lax.axis_size(("sub", "src"))
    hbm = lambda x: pltpu.with_memory_space_constraint(x, pltpu.HBM)
    partial, eig = call(
        functools.partial(correlation_kernel, nev=nev, slices=slices),
        (shape(lat, 8, 128), jax.ShapeDtypeStruct(eig.shape, eig.dtype)),
        3, 226_000_000, hbm=(0, 1), smem=(2,),
        scratch=[
            pltpu.VMEM(src.shape, f32),
            pltpu.SemaphoreType.DMA((slices + 2,)),
        ],
    )(hbm(eig), hbm(src), damping)
    partial = lax.all_to_all(partial, "lat", 0, 0, tiled=True)
    partial = jnp.broadcast_to(partial.sum(0)[None], (rest, 8, 128))
    partial = lax.all_to_all(partial, ("sub", "src"), 0, 0, tiled=True)

    field = shape(slices, comps, 8, 128)
    z_halos = (shape(slices, 12, 8, 128),) * 2
    t_halos = (shape(12, 8, 128),) * 2
    flat = shape(count * comps * slices, 128)
    slab = shape(4 * 18 * slices, 128)
    x, flat_links, rate, guess, znear, zfar, tnear, tfar = call(
        functools.partial(guess_kernel, nev=nev, slices=slices, norm=norm),
        (field, slab, shape(8, 128), pltpu.VMEM(flat.shape, f32)) + z_halos + t_halos,
        4, 226_000_000, hbm=(3,),
        scratch=[pltpu.SemaphoreType.DMA((2,))],
    )(partial, eigvals.reshape(1, nev), eig, hbm(links.reshape(4 * 18 * slices, zdim, 128)))

    time = ("lat", "sub")
    for sweep in range(ITERS):
        final = sweep == ITERS - 1
        znear = swap(znear, "src", False)
        zfar = swap(zfar, "src", True)
        tnear = swap(tnear, time, False)
        tfar = swap(tfar, time, True)
        y = call(
            functools.partial(local_kernel, slices=slices), field, 4,
            10_000_000, scratch=[pltpu.VMEM((12, 8, 128), f32)],
        )(x, src, flat_links, rate)
        if not final:
            next_tnear, next_tfar = call(
                functools.partial(edge_kernel, slices=slices), t_halos, 5, 1_000_000,
            )(y, flat_links, rate, znear, zfar)
        outs = flat if final else (field,) + z_halos
        res = call(
            functools.partial(halo_kernel, slices=slices, final=final),
            outs, 7, 5_000_000,
            scratch=[pltpu.VMEM((2, 12, 8, 128), f32)],
        )(y, flat_links, rate, znear, zfar, tnear, tfar)
        if final:
            x = res
        else:
            x, znear, zfar = res
            tnear, tfar = next_tnear, next_tfar
    return (guess.reshape(sources.shape), x.reshape(sources.shape))


def solution(mesh):
    return jax.shard_map(
        shards,
        mesh=mesh,
        in_specs=(
            P(None, None, ("lat", "sub"), "src", None),
            P(None, None, ("lat", "sub"), "src", None),
            P(),
            P(None, None, ("lat", "sub"), None, None),
            P("src"),
        ),
        out_specs=(
            P(None, None, ("lat", "sub"), "src", None),
            P(None, None, ("lat", "sub"), "src", None),
        ),
        check_vma=False,
    )
```

```python
import functools
import math

import jax
import jax.numpy as jnp
from jax import lax
from jax.experimental import pallas as pl
from jax.experimental.pallas import tpu as pltpu
from jax.sharding import PartitionSpec as P

LX = 16
ITERS = 2
HOPPING = 0.12

BLOCKS = [
    {(0, 1): 1, (1, 0): 1},
    {(0, 1): 2, (1, 0): 0},
    {(0, 0): 1, (1, 1): 3},
    {(0, 0): 0, (1, 1): 0},
]


def times_power(power, re, im):
    return [
        ((1, re), (1, im)),
        ((-1, im), (1, re)),
        ((-1, re), (-1, im)),
        ((1, im), (-1, re)),
    ][power % 4]


def add_signed(base, sign, value):
    return base + value if sign > 0 else base - value


def project(sign, direction, load):
    half = []
    for row in range(2):
        col, power = next((c, p) for (r, c), p in BLOCKS[direction].items() if r == row)
        colours = []
        for colour in range(3):
            lower_re, lower_im = load(0, 2 + col, colour), load(1, 2 + col, colour)
            (sr, vr), (si, vi) = times_power(power, lower_re, lower_im)
            colours.append(
                (
                    add_signed(load(0, row, colour), sr * sign, vr),
                    add_signed(load(1, row, colour), si * sign, vi),
                )
            )
        half.append(colours)
    return half


def rebuild_into(acc, sign, direction, half):
    def put(key, sgn, value):
        if key in acc:
            acc[key] = add_signed(acc[key], sgn, value)
        else:
            acc[key] = value if sgn > 0 else -value

    for row in range(2):
        for colour in range(3):
            re, im = half[row][colour]
            put((0, row, colour), 1, re)
            put((1, row, colour), 1, im)
    for (row, col), power in BLOCKS[direction].items():
        for colour in range(3):
            re, im = half[row][colour]
            (sr, vr), (si, vi) = times_power(-power, re, im)
            put((0, 2 + col, colour), sr * sign, vr)
            put((1, 2 + col, colour), si * sign, vi)


def colour_mul(link, half, adjoint):
    out = []
    for spin in range(2):
        rows = []
        for row in range(3):
            re = im = None
            for col in range(3):
                lr, li = link[(col, row)] if adjoint else link[(row, col)]
                hr, hi = half[spin][col]
                if adjoint:
                    tr, ti = lr * hr + li * hi, lr * hi - li * hr
                else:
                    tr, ti = lr * hr - li * hi, lr * hi + li * hr
                re = tr if re is None else re + tr
                im = ti if im is None else im + ti
            rows.append((re, im))
        out.append(rows)
    return out


def map_half(fn, half):
    return [[(fn(re), fn(im)) for re, im in rows] for rows in half]


def load_half(load):
    return [[(load(3 * s + c), load(6 + 3 * s + c)) for c in range(3)] for s in range(2)]


def store_half(store, half):
    for s in range(2):
        for c in range(3):
            store(3 * s + c, half[s][c][0])
            store(6 + 3 * s + c, half[s][c][1])


def load_link(links_ref, slices, direction, t):
    def one(comp):
        row = (direction * 18 + comp) * slices + t
        return jnp.broadcast_to(links_ref[pl.ds(row, 1), :], (8, 128))

    return {(a, c): (one(3 * a + c), one(9 + 3 * a + c)) for a in range(3) for c in range(3)}


def moved(direction, step):
    def fn(v):
        if direction == 1:
            return pltpu.roll(v, (-step * LX) % 128, 1)
        column = lax.rem(lax.broadcasted_iota(jnp.int32, v.shape, 1), LX)
        border = LX - 1 if step > 0 else 0
        inside = pltpu.roll(v, (-step) % 128, 1)
        wrapped = pltpu.roll(v, (step * (LX - 1)) % 128, 1)
        return jnp.where(column == border, wrapped, inside)

    return fn


def correlation_kernel(
    eig_hbm, src_hbm, links_hbm, damp_ref, out_ref, eig_ref, links_ref, src_ref, sems, *, nev, slices
):
    comps = 24
    sources = 8
    rows = sources * comps * slices // 2
    src_copies = [
        pltpu.make_async_copy(
            src_hbm.at[pl.ds(i * rows, rows)], src_ref.at[pl.ds(i * rows, rows)], sems.at[slices + i]
        )
        for i in range(2)
    ]
    eig_copies = [
        pltpu.make_async_copy(eig_hbm.at[:, t], eig_ref.at[:, t], sems.at[t]) for t in range(slices)
    ]
    links_copy = pltpu.make_async_copy(
        links_hbm.at[:, lax.axis_index("src")], links_ref, sems.at[slices + 2]
    )
    for copy in src_copies + eig_copies + [links_copy]:
        copy.start()
    for copy in src_copies:
        copy.wait()
    full = jnp.zeros((sources * comps, nev * comps), jnp.float32)
    for t in range(0, slices, 2):
        lhs = [
            src_ref[pl.ds(u, sources * comps, stride=slices), :].astype(jnp.bfloat16)
            for u in (t, t + 1)
        ]
        eig_copies[t].wait()
        eig_copies[t + 1].wait()
        rhs = [eig_ref[:, u].reshape(nev * comps, 128) for u in (t, t + 1)]
        full = full + lax.dot_general(
            jnp.concatenate(lhs, axis=1), jnp.concatenate(rhs, axis=1),
            (((1,), (1,)), ((), ())), preferred_element_type=jnp.float32,
        )
    row = lax.rem(lax.broadcasted_iota(jnp.int32, (sources * comps, 1), 0), comps)
    col = lax.rem(lax.broadcasted_iota(jnp.int32, (1, nev * comps), 1), comps)
    gap = row - col
    straight = jnp.where(gap == 0, full, 0.0)
    crossed = jnp.where(gap == 12, full, 0.0) - jnp.where(gap == -12, full, 0.0)
    straight = straight.reshape(sources, comps, nev * comps).sum(1)
    crossed = crossed.reshape(sources, comps, nev * comps).sum(1)
    both = jnp.concatenate([straight, crossed], axis=0)
    high = both.astype(jnp.bfloat16)
    middle = (both - high.astype(jnp.float32)).astype(jnp.bfloat16)
    low = (both - high.astype(jnp.float32) - middle.astype(jnp.float32)).astype(jnp.bfloat16)
    parts = jnp.concatenate([high, middle, low], axis=0)
    first = lax.broadcasted_iota(jnp.int32, (nev * comps, 128), 0)
    start = lax.broadcasted_iota(jnp.int32, (nev * comps, 128), 1) * comps
    gather = jnp.where((first >= start) & (first < start + comps), 1.0, 0.0).astype(jnp.bfloat16)
    sums = jnp.dot(parts, gather, preferred_element_type=jnp.float32)
    sums = (sums[0:16] + sums[16:32]) + sums[32:48]
    total = sums[0:8] + pltpu.roll(sums[8:16], nev, 1)
    links_copy.wait()
    holder = (lax.axis_index("lat") == 0) & (lax.axis_index("sub") == 0)
    value = jnp.where(holder, damp_ref[0], 0.0)
    at_row = lax.broadcasted_iota(jnp.int32, (8, 128), 0) == lax.axis_index("src")
    at_lane = lax.broadcasted_iota(jnp.int32, (8, 128), 1) == 2 * nev
    total = total + jnp.where(at_row & at_lane, value, 0.0)
    out_ref[...] = jnp.broadcast_to(total[None], out_ref.shape)


def choose(flag, half_true, half_false):
    return [
        [
            tuple(jnp.where(flag, a, b) for a, b in zip(half_true[s][c], half_false[s][c]))
            for c in range(3)
        ]
        for s in range(2)
    ]


def z_even():
    return lax.rem(lax.axis_index("src"), 2) == 0


def t_place():
    place = lax.axis_index(("lat", "sub"))
    return place, lax.rem(place, 2) == 0


def emit_halos(load, links_ref, t, near_ref, far_ref, slices):
    even = z_even()
    up = project(1, 2, load)
    up = colour_mul(load_link(links_ref, slices, 2, t), up, True)
    down = project(-1, 2, load)
    store_half(lambda i, v: near_ref.__setitem__((t, i), v), choose(even, up, down))
    store_half(lambda i, v: far_ref.__setitem__((t, i), v), choose(even, down, up))


def emit_time_halos(load_last, load_first, links_ref, near_ref, far_ref, slices):
    place, even = t_place()
    extent = lax.axis_size(("lat", "sub"))
    up_sign = jnp.where(place == extent - 1, -1.0, 1.0)
    down_sign = jnp.where(place == 0, -1.0, 1.0)
    last = slices - 1
    up = project(1, 3, load_last)
    up = colour_mul(load_link(links_ref, slices, 3, last), up, True)
    up = map_half(lambda v: v * up_sign, up)
    down = project(-1, 3, load_first)
    down = map_half(lambda v: v * down_sign, down)
    store_half(lambda i, v: near_ref.__setitem__(i, v), choose(even, up, down))
    store_half(lambda i, v: far_ref.__setitem__(i, v), choose(even, down, up))


def guess_kernel(
    part_ref, ev_ref, eig_ref, links_ref,
    x_ref, rate_ref, guess_ref, znear_ref, zfar_ref, tnear_ref, tfar_ref,
    *, nev, slices, norm,
):
    comps = 24
    total = part_ref[0]
    for i in range(1, part_ref.shape[0]):
        total = total + part_ref[i]
    ev = ev_ref[...]
    w_re = ((total[:, :nev] / norm) / ev).astype(jnp.bfloat16)
    w_im = ((total[:, nev : 2 * nev] / norm) / ev).astype(jnp.bfloat16)
    rate_ref[...] = jnp.broadcast_to(total[:, 2 * nev : 2 * nev + 1], (8, 128))
    row = lax.broadcasted_iota(jnp.int32, (nev, nev * comps), 0) * comps
    col = lax.broadcasted_iota(jnp.int32, (nev, nev * comps), 1)
    spread = jnp.where((col >= row) & (col < row + comps), 1.0, 0.0).astype(jnp.bfloat16)
    w_re = jnp.dot(w_re, spread, preferred_element_type=jnp.float32)
    w_im = jnp.dot(w_im, spread, preferred_element_type=jnp.float32)
    comp = lax.rem(lax.broadcasted_iota(jnp.int32, (8, nev * comps), 1), comps)
    blocks = []
    for c in range(comps):
        other, turned = (c + 12, -w_im) if c < 12 else (c - 12, w_im)
        blocks.append(jnp.where(comp == c, w_re, jnp.where(comp == other, turned, 0.0)))
    mix = jnp.concatenate(blocks, axis=0).astype(jnp.bfloat16)
    for t in range(slices):
        res = jnp.dot(
            mix, eig_ref[:, t].reshape(nev * comps, 128), preferred_element_type=jnp.float32
        )
        x_ref[t] = res.reshape(comps, 8, 128)

    def step(t, carry):
        for c in range(comps):
            guess_ref[pl.ds(c * slices + t, 8, stride=comps * slices), :] = x_ref[t, c]
        emit_halos(
            lambda p, s, c: x_ref[t, 12 * p + 3 * s + c],
            links_ref, t, znear_ref, zfar_ref, slices,
        )
        return carry

    lax.fori_loop(0, slices, step, 0)
    load = lambda t: lambda p, s, c: x_ref[t, 12 * p + 3 * s + c]
    emit_time_halos(load(slices - 1), load(0), links_ref, tnear_ref, tfar_ref, slices)


def local_kernel(x_ref, src_ref, links_ref, rate_ref, y_ref, behind_ref, *, slices):
    behind_ref[...] = jnp.zeros_like(behind_ref)

    def step(t, carry):
        load = lambda p, s, c: x_ref[t, 12 * p + 3 * s + c]
        acc = {}
        for direction in range(2):
            link = load_link(links_ref, slices, direction, t)
            ahead = map_half(moved(direction, 1), project(-1, direction, load))
            rebuild_into(acc, -1, direction, colour_mul(link, ahead, False))
            behind = colour_mul(link, project(1, direction, load), True)
            rebuild_into(acc, 1, direction, map_half(moved(direction, -1), behind))
        link = load_link(links_ref, slices, 3, t)
        inside = jnp.where(t == slices - 1, 0.0, 1.0)
        following = jnp.minimum(t + 1, slices - 1)
        ahead = project(-1, 3, lambda p, s, c: x_ref[following, 12 * p + 3 * s + c])
        ahead = map_half(lambda v: v * inside, ahead)
        rebuild_into(acc, -1, 3, colour_mul(link, ahead, False))
        rebuild_into(acc, 1, 3, load_half(lambda i: behind_ref[i]))
        up = colour_mul(link, project(1, 3, load), True)
        store_half(lambda i, v: behind_ref.__setitem__(i, v), up)
        rate = rate_ref[...]
        for (p, s, c), hop in acc.items():
            comp = 12 * p + 3 * s + c
            where = pl.ds(comp * slices + t, 8, stride=24 * slices)
            value = load(p, s, c)
            y_ref[t, comp] = value + rate * (src_ref[where, :] - (value - HOPPING * hop))
        return carry

    lax.fori_loop(0, slices, step, 0)


def z_hops(links_ref, znear_ref, zfar_ref, t, slices):
    above_near = z_even()
    acc = {}
    near, far = (load_half(lambda i, ref=ref: ref[t, i]) for ref in (znear_ref, zfar_ref))
    link = load_link(links_ref, slices, 2, t)
    rebuild_into(acc, -1, 2, colour_mul(link, choose(above_near, near, far), False))
    rebuild_into(acc, 1, 2, choose(above_near, far, near))
    return acc


def edge_kernel(y_ref, links_ref, rate_ref, znear_ref, zfar_ref, tnear_ref, tfar_ref, *, slices):
    rate = rate_ref[...] * HOPPING

    def load(t):
        hops = z_hops(links_ref, znear_ref, zfar_ref, t, slices)
        return lambda p, s, c: y_ref[t, 12 * p + 3 * s + c] + rate * hops[(p, s, c)]

    emit_time_halos(load(slices - 1), load(0), links_ref, tnear_ref, tfar_ref, slices)


def halo_kernel(
    y_ref, links_ref, rate_ref, znear_ref, zfar_ref, tnear_ref, tfar_ref, *refs, slices, final
):
    _, t_even = t_place()
    edge_ref = refs[-1]
    last = slices - 1
    near, far = (load_half(lambda i, ref=ref: ref[i]) for ref in (tnear_ref, tfar_ref))
    link = load_link(links_ref, slices, 3, last)
    above = colour_mul(link, choose(t_even, near, far), False)
    store_half(lambda i, v: edge_ref.__setitem__((0, i), v), above)
    store_half(lambda i, v: edge_ref.__setitem__((1, i), v), choose(t_even, far, near))

    def step(t, carry):
        acc = z_hops(links_ref, znear_ref, zfar_ref, t, slices)
        top, bottom = (jnp.where(t == edge, 1.0, 0.0) for edge in (last, 0))
        rebuild_into(acc, -1, 3, map_half(lambda v: v * top, load_half(lambda i: edge_ref[0, i])))
        rebuild_into(acc, 1, 3, map_half(lambda v: v * bottom, load_half(lambda i: edge_ref[1, i])))
        rate = rate_ref[...] * HOPPING
        new = {}
        for (p, s, c), hop in acc.items():
            comp = 12 * p + 3 * s + c
            value = y_ref[t, comp] + rate * hop
            new[(p, s, c)] = value
            if final:
                refs[0][pl.ds(comp * slices + t, 8, stride=24 * slices), :] = value
            else:
                refs[0][t, comp] = value
        if not final:
            emit_halos(
                lambda p, s, c: new[(p, s, c)], links_ref, t, refs[1], refs[2], slices
            )
        return carry

    lax.fori_loop(0, slices, step, 0)


def call(kernel, outs, ins, flops, hbm=(), smem=(), scratch=()):
    space = lambda i: pltpu.HBM if i in hbm else pltpu.SMEM if i in smem else pltpu.VMEM
    return pl.pallas_call(
        kernel,
        out_shape=outs,
        in_specs=[pl.BlockSpec(memory_space=space(i)) for i in range(ins)],
        out_specs=jax.tree.map(lambda _: pl.BlockSpec(memory_space=pltpu.VMEM), outs),
        scratch_shapes=list(scratch),
        compiler_params=pltpu.CompilerParams(vmem_limit_bytes=24 << 20),
        cost_estimate=pl.CostEstimate(
            flops=flops, bytes_accessed=3_000_000, transcendentals=0
        ),
    )


def swap(x, axis, far):
    n = lax.axis_size(axis)
    partner = lambda i: (i + 1 if i % 2 else i - 1) % n if far else i ^ 1
    return lax.ppermute(x, axis, [(i, partner(i)) for i in range(n)])


def shards(sources, eigvecs, eigvals, links, damping):
    count, comps, slices = sources.shape[:3]
    nev = eigvecs.shape[0]
    zdim = links.shape[3]
    devices = lax.axis_size(("src", "lat", "sub"))
    norm = math.sqrt(comps * slices * 128 * devices)
    f32 = jnp.float32

    src = sources.reshape(count * comps * slices, 128)
    eig = eigvecs.transpose(0, 2, 3, 1, 4).reshape(nev, slices, comps, 128)

    shape = lambda *dims: jax.ShapeDtypeStruct(dims, f32)
    lat, rest = lax.axis_size("lat"), lax.axis_size(("sub", "src"))
    hbm = lambda x: pltpu.with_memory_space_constraint(x, pltpu.HBM)
    slab = shape(4 * 18 * slices, 128)
    partial, eig, flat_links = call(
        functools.partial(correlation_kernel, nev=nev, slices=slices),
        (shape(lat, 8, 128), jax.ShapeDtypeStruct(eig.shape, eig.dtype), slab),
        4, 226_000_000, hbm=(0, 1, 2), smem=(3,),
        scratch=[
            pltpu.VMEM(src.shape, f32),
            pltpu.SemaphoreType.DMA((slices + 3,)),
        ],
    )(hbm(eig), hbm(src), hbm(links.reshape(4 * 18 * slices, zdim, 128)), damping)
    partial = lax.all_to_all(partial, "lat", 0, 0, tiled=True)
    partial = jnp.broadcast_to(partial.sum(0)[None], (rest, 8, 128))
    partial = lax.all_to_all(partial, ("sub", "src"), 0, 0, tiled=True)

    field = shape(slices, comps, 8, 128)
    z_halos = (shape(slices, 12, 8, 128),) * 2
    t_halos = (shape(12, 8, 128),) * 2
    flat = shape(count * comps * slices, 128)
    x, rate, guess, znear, zfar, tnear, tfar = call(
        functools.partial(guess_kernel, nev=nev, slices=slices, norm=norm),
        (field, shape(8, 128), pltpu.VMEM(flat.shape, f32)) + z_halos + t_halos,
        4, 226_000_000,
    )(partial, eigvals.reshape(1, nev), eig, flat_links)

    time = ("lat", "sub")
    for sweep in range(ITERS):
        final = sweep == ITERS - 1
        znear = swap(znear, "src", False)
        zfar = swap(zfar, "src", True)
        tnear = swap(tnear, time, False)
        tfar = swap(tfar, time, True)
        y = call(
            functools.partial(local_kernel, slices=slices), field, 4,
            10_000_000, scratch=[pltpu.VMEM((12, 8, 128), f32)],
        )(x, src, flat_links, rate)
        if not final:
            next_tnear, next_tfar = call(
                functools.partial(edge_kernel, slices=slices), t_halos, 5, 1_000_000,
            )(y, flat_links, rate, znear, zfar)
        outs = flat if final else (field,) + z_halos
        res = call(
            functools.partial(halo_kernel, slices=slices, final=final),
            outs, 7, 5_000_000,
            scratch=[pltpu.VMEM((2, 12, 8, 128), f32)],
        )(y, flat_links, rate, znear, zfar, tnear, tfar)
        if final:
            x = res
        else:
            x, znear, zfar = res
            tnear, tfar = next_tnear, next_tfar
    return (guess.reshape(sources.shape), x.reshape(sources.shape))


def solution(mesh):
    return jax.shard_map(
        shards,
        mesh=mesh,
        in_specs=(
            P(None, None, ("lat", "sub"), "src", None),
            P(None, None, ("lat", "sub"), "src", None),
            P(),
            P(None, None, ("lat", "sub"), None, None),
            P("src"),
        ),
        out_specs=(
            P(None, None, ("lat", "sub"), "src", None),
            P(None, None, ("lat", "sub"), "src", None),
        ),
        check_vma=False,
    )
```

```python
import functools
import math

import jax
import jax.numpy as jnp
from jax import lax
from jax.experimental import pallas as pl
from jax.experimental.pallas import tpu as pltpu
from jax.sharding import PartitionSpec as P

LX = 16
HOPPING = 0.12

BLOCKS = [
    {(0, 1): 1, (1, 0): 1},
    {(0, 1): 2, (1, 0): 0},
    {(0, 0): 1, (1, 1): 3},
    {(0, 0): 0, (1, 1): 0},
]


def times_power(power, re, im):
    return [
        ((1, re), (1, im)),
        ((-1, im), (1, re)),
        ((-1, re), (-1, im)),
        ((1, im), (-1, re)),
    ][power % 4]


def add_signed(base, sign, value):
    return base + value if sign > 0 else base - value


def project(sign, direction, load):
    half = []
    for row in range(2):
        col, power = next((c, p) for (r, c), p in BLOCKS[direction].items() if r == row)
        colours = []
        for colour in range(3):
            lower_re, lower_im = load(0, 2 + col, colour), load(1, 2 + col, colour)
            (sr, vr), (si, vi) = times_power(power, lower_re, lower_im)
            colours.append(
                (
                    add_signed(load(0, row, colour), sr * sign, vr),
                    add_signed(load(1, row, colour), si * sign, vi),
                )
            )
        half.append(colours)
    return half


def rebuild_into(acc, sign, direction, half):
    def put(key, sgn, value):
        if key in acc:
            acc[key] = add_signed(acc[key], sgn, value)
        else:
            acc[key] = value if sgn > 0 else -value

    for row in range(2):
        for colour in range(3):
            re, im = half[row][colour]
            put((0, row, colour), 1, re)
            put((1, row, colour), 1, im)
    for (row, col), power in BLOCKS[direction].items():
        for colour in range(3):
            re, im = half[row][colour]
            (sr, vr), (si, vi) = times_power(-power, re, im)
            put((0, 2 + col, colour), sr * sign, vr)
            put((1, 2 + col, colour), si * sign, vi)


def colour_mul(link, half, adjoint):
    out = []
    for spin in range(2):
        rows = []
        for row in range(3):
            re = im = None
            for col in range(3):
                lr, li = link[(col, row)] if adjoint else link[(row, col)]
                hr, hi = half[spin][col]
                if adjoint:
                    tr, ti = lr * hr + li * hi, lr * hi - li * hr
                else:
                    tr, ti = lr * hr - li * hi, lr * hi + li * hr
                re = tr if re is None else re + tr
                im = ti if im is None else im + ti
            rows.append((re, im))
        out.append(rows)
    return out


def map_half(fn, half):
    return [[(fn(re), fn(im)) for re, im in rows] for rows in half]


def load_half(load):
    return [[(load(3 * s + c), load(6 + 3 * s + c)) for c in range(3)] for s in range(2)]


def store_half(store, half):
    for s in range(2):
        for c in range(3):
            store(3 * s + c, half[s][c][0])
            store(6 + 3 * s + c, half[s][c][1])


def load_link(links_ref, slices, direction, t):
    def one(comp):
        row = (direction * 18 + comp) * slices + t
        return jnp.broadcast_to(links_ref[pl.ds(row, 1), :], (8, 128))

    return {(a, c): (one(3 * a + c), one(9 + 3 * a + c)) for a in range(3) for c in range(3)}


def moved(direction, step):
    def fn(v):
        if direction == 1:
            return pltpu.roll(v, (-step * LX) % 128, 1)
        column = lax.rem(lax.broadcasted_iota(jnp.int32, v.shape, 1), LX)
        border = LX - 1 if step > 0 else 0
        inside = pltpu.roll(v, (-step) % 128, 1)
        wrapped = pltpu.roll(v, (step * (LX - 1)) % 128, 1)
        return jnp.where(column == border, wrapped, inside)

    return fn


def correlation_kernel(
    eig_hbm, src_hbm, links_hbm, damp_ref, out_ref, eig_ref, links_ref, src_ref, sems, *, nev, slices
):
    comps = 24
    sources = 8
    rows = sources * comps * slices // 2
    src_copies = [
        pltpu.make_async_copy(
            src_hbm.at[pl.ds(i * rows, rows)], src_ref.at[pl.ds(i * rows, rows)], sems.at[slices + i]
        )
        for i in range(2)
    ]
    eig_copies = [
        pltpu.make_async_copy(eig_hbm.at[:, t], eig_ref.at[:, t], sems.at[t]) for t in range(slices)
    ]
    links_copy = pltpu.make_async_copy(
        links_hbm.at[:, lax.axis_index("src")], links_ref, sems.at[slices + 2]
    )
    for copy in src_copies + eig_copies + [links_copy]:
        copy.start()
    for copy in src_copies:
        copy.wait()
    full = jnp.zeros((sources * comps, nev * comps), jnp.float32)
    for t in range(0, slices, 2):
        lhs = [
            src_ref[pl.ds(u, sources * comps, stride=slices), :].astype(jnp.bfloat16)
            for u in (t, t + 1)
        ]
        eig_copies[t].wait()
        eig_copies[t + 1].wait()
        rhs = [eig_ref[:, u].reshape(nev * comps, 128) for u in (t, t + 1)]
        full = full + lax.dot_general(
            jnp.concatenate(lhs, axis=1), jnp.concatenate(rhs, axis=1),
            (((1,), (1,)), ((), ())), preferred_element_type=jnp.float32,
        )
    row = lax.rem(lax.broadcasted_iota(jnp.int32, (sources * comps, 1), 0), comps)
    col = lax.rem(lax.broadcasted_iota(jnp.int32, (1, nev * comps), 1), comps)
    gap = row - col
    straight = jnp.where(gap == 0, full, 0.0)
    crossed = jnp.where(gap == 12, full, 0.0) - jnp.where(gap == -12, full, 0.0)
    straight = straight.reshape(sources, comps, nev * comps).sum(1)
    crossed = crossed.reshape(sources, comps, nev * comps).sum(1)
    both = jnp.concatenate([straight, crossed], axis=0)
    high = both.astype(jnp.bfloat16)
    middle = (both - high.astype(jnp.float32)).astype(jnp.bfloat16)
    low = (both - high.astype(jnp.float32) - middle.astype(jnp.float32)).astype(jnp.bfloat16)
    parts = jnp.concatenate([high, middle, low], axis=0)
    first = lax.broadcasted_iota(jnp.int32, (nev * comps, 128), 0)
    start = lax.broadcasted_iota(jnp.int32, (nev * comps, 128), 1) * comps
    gather = jnp.where((first >= start) & (first < start + comps), 1.0, 0.0).astype(jnp.bfloat16)
    sums = jnp.dot(parts, gather, preferred_element_type=jnp.float32)
    sums = (sums[0:16] + sums[16:32]) + sums[32:48]
    total = sums[0:8] + pltpu.roll(sums[8:16], nev, 1)
    links_copy.wait()
    holder = (lax.axis_index("lat") == 0) & (lax.axis_index("sub") == 0)
    value = jnp.where(holder, damp_ref[0], 0.0)
    at_row = lax.broadcasted_iota(jnp.int32, (8, 128), 0) == lax.axis_index("src")
    at_lane = lax.broadcasted_iota(jnp.int32, (8, 128), 1) == 2 * nev
    total = total + jnp.where(at_row & at_lane, value, 0.0)
    out_ref[...] = jnp.broadcast_to(total[None], out_ref.shape)


def choose(flag, half_true, half_false):
    return [
        [
            tuple(jnp.where(flag, a, b) for a, b in zip(half_true[s][c], half_false[s][c]))
            for c in range(3)
        ]
        for s in range(2)
    ]


def z_even():
    return lax.rem(lax.axis_index("src"), 2) == 0


def t_place():
    place = lax.axis_index(("lat", "sub"))
    return place, lax.rem(place, 2) == 0


def emit_halos(load, links_ref, t, near_ref, far_ref, slices, near_t=None, far_t=None):
    even = z_even()
    up = project(1, 2, load)
    up = colour_mul(load_link(links_ref, slices, 2, t), up, True)
    down = project(-1, 2, load)
    near_t, far_t = (t if place is None else place for place in (near_t, far_t))
    store_half(lambda i, v: near_ref.__setitem__((near_t, i), v), choose(even, up, down))
    store_half(lambda i, v: far_ref.__setitem__((far_t, i), v), choose(even, down, up))


def emit_time_halos(load_last, load_first, links_ref, near_ref, far_ref, slices):
    place, even = t_place()
    extent = lax.axis_size(("lat", "sub"))
    up_sign = jnp.where(place == extent - 1, -1.0, 1.0)
    down_sign = jnp.where(place == 0, -1.0, 1.0)
    last = slices - 1
    up = project(1, 3, load_last)
    up = colour_mul(load_link(links_ref, slices, 3, last), up, True)
    up = map_half(lambda v: v * up_sign, up)
    down = project(-1, 3, load_first)
    down = map_half(lambda v: v * down_sign, down)
    store_half(lambda i, v: near_ref.__setitem__(i, v), choose(even, up, down))
    store_half(lambda i, v: far_ref.__setitem__(i, v), choose(even, down, up))


def guess_kernel(
    part_ref, ev_ref, eig_ref, links_ref,
    x_ref, rate_ref, guess_ref, znear_ref, zfar_ref, tnear_ref, tfar_ref,
    *, nev, slices, norm,
):
    comps = 24
    total = part_ref[0]
    for i in range(1, part_ref.shape[0]):
        total = total + part_ref[i]
    ev = ev_ref[...]
    w_re = ((total[:, :nev] / norm) / ev).astype(jnp.bfloat16)
    w_im = ((total[:, nev : 2 * nev] / norm) / ev).astype(jnp.bfloat16)
    rate_ref[...] = jnp.broadcast_to(total[:, 2 * nev : 2 * nev + 1], (8, 128))
    row = lax.broadcasted_iota(jnp.int32, (nev, nev * comps), 0) * comps
    col = lax.broadcasted_iota(jnp.int32, (nev, nev * comps), 1)
    spread = jnp.where((col >= row) & (col < row + comps), 1.0, 0.0).astype(jnp.bfloat16)
    w_re = jnp.dot(w_re, spread, preferred_element_type=jnp.float32)
    w_im = jnp.dot(w_im, spread, preferred_element_type=jnp.float32)
    comp = lax.rem(lax.broadcasted_iota(jnp.int32, (8, nev * comps), 1), comps)
    blocks = []
    for c in range(comps):
        other, turned = (c + 12, -w_im) if c < 12 else (c - 12, w_im)
        blocks.append(jnp.where(comp == c, w_re, jnp.where(comp == other, turned, 0.0)))
    mix = jnp.concatenate(blocks, axis=0).astype(jnp.bfloat16)
    for t in range(slices):
        res = jnp.dot(
            mix, eig_ref[:, t].reshape(nev * comps, 128), preferred_element_type=jnp.float32
        )
        x_ref[t] = res.reshape(comps, 8, 128)

    def step(t, carry):
        for c in range(comps):
            guess_ref[pl.ds(c * slices + t, 8, stride=comps * slices), :] = x_ref[t, c]
        emit_halos(
            lambda p, s, c: x_ref[t, 12 * p + 3 * s + c],
            links_ref, t, znear_ref, zfar_ref, slices,
        )
        return carry

    lax.fori_loop(0, slices, step, 0)
    load = lambda t: lambda p, s, c: x_ref[t, 12 * p + 3 * s + c]
    emit_time_halos(load(slices - 1), load(0), links_ref, tnear_ref, tfar_ref, slices)


def local_kernel(x_ref, src_ref, links_ref, rate_ref, y_ref, behind_ref, *, slices):
    behind_ref[...] = jnp.zeros_like(behind_ref)

    def step(t, carry):
        load = lambda p, s, c: x_ref[t, 12 * p + 3 * s + c]
        acc = {}
        for direction in range(2):
            link = load_link(links_ref, slices, direction, t)
            ahead = map_half(moved(direction, 1), project(-1, direction, load))
            rebuild_into(acc, -1, direction, colour_mul(link, ahead, False))
            behind = colour_mul(link, project(1, direction, load), True)
            rebuild_into(acc, 1, direction, map_half(moved(direction, -1), behind))
        link = load_link(links_ref, slices, 3, t)
        inside = jnp.where(t == slices - 1, 0.0, 1.0)
        following = jnp.minimum(t + 1, slices - 1)
        ahead = project(-1, 3, lambda p, s, c: x_ref[following, 12 * p + 3 * s + c])
        ahead = map_half(lambda v: v * inside, ahead)
        rebuild_into(acc, -1, 3, colour_mul(link, ahead, False))
        rebuild_into(acc, 1, 3, load_half(lambda i: behind_ref[i]))
        up = colour_mul(link, project(1, 3, load), True)
        store_half(lambda i, v: behind_ref.__setitem__(i, v), up)
        rate = rate_ref[...]
        for (p, s, c), hop in acc.items():
            comp = 12 * p + 3 * s + c
            where = pl.ds(comp * slices + t, 8, stride=24 * slices)
            value = load(p, s, c)
            y_ref[t, comp] = value + rate * (src_ref[where, :] - (value - HOPPING * hop))
        return carry

    lax.fori_loop(0, slices, step, 0)


def z_hops(links_ref, znear_ref, zfar_ref, t, slices, far_t=None):
    above_near = z_even()
    acc = {}
    far_t = t if far_t is None else far_t
    near = load_half(lambda i: znear_ref[t, i])
    far = load_half(lambda i: zfar_ref[far_t, i])
    link = load_link(links_ref, slices, 2, t)
    rebuild_into(acc, -1, 2, colour_mul(link, choose(above_near, near, far), False))
    rebuild_into(acc, 1, 2, choose(above_near, far, near))
    return acc


def edge_kernel(
    y_ref, links_ref, rate_ref, znear_ref, zfar_ref, first_ref, tnear_ref, tfar_ref, *, slices
):
    rate = rate_ref[...] * HOPPING

    def load(t):
        hops = z_hops(links_ref, znear_ref, zfar_ref, t, slices)
        return lambda p, s, c: y_ref[t, 12 * p + 3 * s + c] + rate * hops[(p, s, c)]

    tfar_ref[0] = first_ref[...]
    emit_time_halos(load(slices - 1), load(0), links_ref, tnear_ref, tfar_ref.at[1], slices)


def inner_kernel(
    y_ref, links_ref, rate_ref, znear_ref, zfar_ref, x_ref, near_ref, far_ref, *, slices
):
    def step(t, carry):
        rate = rate_ref[...] * HOPPING
        new = {}
        for (p, s, c), hop in z_hops(links_ref, znear_ref, zfar_ref, t, slices).items():
            comp = 12 * p + 3 * s + c
            new[(p, s, c)] = y_ref[t, comp] + rate * hop
            x_ref[t - 1, comp] = new[(p, s, c)]
        emit_halos(
            lambda p, s, c: new[(p, s, c)], links_ref, t, near_ref, far_ref, slices, t - 1, t - 1
        )
        return carry

    lax.fori_loop(1, slices - 1, step, 0)


def t_hops(links_ref, tnear_ref, tfar_ref, slices):
    _, even = t_place()
    near, far = (load_half(lambda i, ref=ref: ref[i]) for ref in (tnear_ref, tfar_ref))
    first, last = {}, {}
    rebuild_into(first, 1, 3, choose(even, far, near))
    link = load_link(links_ref, slices, 3, slices - 1)
    rebuild_into(last, -1, 3, colour_mul(link, choose(even, near, far), False))
    return first, last


def outer_kernel(
    y_ref, links_ref, rate_ref, znear_ref, zfar_ref, tnear_ref, tfar_ref, inner_x_ref, inner_near_ref,
    x_ref, near_ref, far_ref, *, slices,
):
    x_ref[1 : slices - 1] = inner_x_ref[...]
    near_ref[1 : slices - 1] = inner_near_ref[...]
    rate = rate_ref[...] * HOPPING
    for i, hops in enumerate(t_hops(links_ref, tnear_ref, tfar_ref.at[0], slices)):
        t = (slices - 1) * i
        new = {}
        for (p, s, c), hop in z_hops(links_ref, znear_ref, zfar_ref, t, slices).items():
            comp = 12 * p + 3 * s + c
            new[(p, s, c)] = y_ref[t, comp] + rate * (hop + hops[(p, s, c)])
            x_ref[t, comp] = new[(p, s, c)]
        emit_halos(
            lambda p, s, c: new[(p, s, c)], links_ref, t, near_ref, far_ref, slices, t, i
        )


def last_kernel(
    y_ref, links_ref, rate_ref, znear_ref, zinner_ref, zouter_ref, tnear_ref, tfar_ref, out_ref, *, slices
):
    rate = rate_ref[...] * HOPPING

    def finish(t, hops, more=None):
        for key, hop in hops.items():
            p, s, c = key
            comp = 12 * p + 3 * s + c
            hop = hop if more is None else hop + more[key]
            where = pl.ds(comp * slices + t, 8, stride=24 * slices)
            out_ref[where, :] = y_ref[t, comp] + rate * hop

    for i, more in enumerate(t_hops(links_ref, tnear_ref, tfar_ref.at[1], slices)):
        t = (slices - 1) * i
        finish(t, z_hops(links_ref, znear_ref, zouter_ref, t, slices, i), more)

    def step(t, carry):
        finish(t, z_hops(links_ref, znear_ref, zinner_ref, t, slices, t - 1))
        return carry

    lax.fori_loop(1, slices - 1, step, 0)


def call(kernel, outs, ins, flops, hbm=(), smem=(), scratch=()):
    space = lambda i: pltpu.HBM if i in hbm else pltpu.SMEM if i in smem else pltpu.VMEM
    return pl.pallas_call(
        kernel,
        out_shape=outs,
        in_specs=[pl.BlockSpec(memory_space=space(i)) for i in range(ins)],
        out_specs=jax.tree.map(lambda _: pl.BlockSpec(memory_space=pltpu.VMEM), outs),
        scratch_shapes=list(scratch),
        compiler_params=pltpu.CompilerParams(vmem_limit_bytes=24 << 20),
        cost_estimate=pl.CostEstimate(
            flops=flops, bytes_accessed=3_000_000, transcendentals=0
        ),
    )


def swap(x, axis, far):
    n = lax.axis_size(axis)
    partner = lambda i: (i + 1 if i % 2 else i - 1) % n if far else i ^ 1
    return lax.ppermute(x, axis, [(i, partner(i)) for i in range(n)])


def shards(sources, eigvecs, eigvals, links, damping):
    count, comps, slices = sources.shape[:3]
    nev = eigvecs.shape[0]
    zdim = links.shape[3]
    devices = lax.axis_size(("src", "lat", "sub"))
    norm = math.sqrt(comps * slices * 128 * devices)
    f32 = jnp.float32

    src = sources.reshape(count * comps * slices, 128)
    eig = eigvecs.transpose(0, 2, 3, 1, 4).reshape(nev, slices, comps, 128)

    shape = lambda *dims: jax.ShapeDtypeStruct(dims, f32)
    lat, rest = lax.axis_size("lat"), lax.axis_size(("sub", "src"))
    hbm = lambda x: pltpu.with_memory_space_constraint(x, pltpu.HBM)
    slab = shape(4 * 18 * slices, 128)
    partial, eig, flat_links = call(
        functools.partial(correlation_kernel, nev=nev, slices=slices),
        (shape(lat, 8, 128), jax.ShapeDtypeStruct(eig.shape, eig.dtype), slab),
        4, 226_000_000, hbm=(0, 1, 2), smem=(3,),
        scratch=[
            pltpu.VMEM(src.shape, f32),
            pltpu.SemaphoreType.DMA((slices + 3,)),
        ],
    )(hbm(eig), hbm(src), hbm(links.reshape(4 * 18 * slices, zdim, 128)), damping)
    partial = lax.all_to_all(partial, "lat", 0, 0, tiled=True)
    partial = jnp.broadcast_to(partial.sum(0)[None], (rest, 8, 128))
    partial = lax.all_to_all(partial, ("sub", "src"), 0, 0, tiled=True)

    field = shape(slices, comps, 8, 128)
    z_halos = (shape(slices, 12, 8, 128),) * 2
    t_halos = (shape(12, 8, 128),) * 2
    flat = shape(count * comps * slices, 128)
    x, rate, guess, znear, zfar, tnear, tfar = call(
        functools.partial(guess_kernel, nev=nev, slices=slices, norm=norm),
        (field, shape(8, 128), pltpu.VMEM(flat.shape, f32)) + z_halos + t_halos,
        4, 226_000_000,
    )(partial, eigvals.reshape(1, nev), eig, flat_links)

    time = ("lat", "sub")

    def stage(kernel, outs, *args, scratch=()):
        return call(
            functools.partial(kernel, slices=slices), outs, len(args),
            5_000_000, scratch=scratch,
        )(*args)

    carry = [pltpu.VMEM((12, 8, 128), f32)]
    zfar = swap(zfar, "src", True)
    znear = swap(znear, "src", False)
    tnear = swap(tnear, time, False)
    y = stage(local_kernel, field, x, src, flat_links, rate, scratch=carry)
    next_tnear, both_tfar = stage(
        edge_kernel, (shape(12, 8, 128), shape(2, 12, 8, 128)),
        y, flat_links, rate, znear, zfar, tfar,
    )
    both_tfar = swap(both_tfar, time, True)
    inner = slices - 2
    inner_x, inner_near, zinner = stage(
        inner_kernel,
        (shape(inner, comps, 8, 128), shape(inner, 12, 8, 128), shape(inner, 12, 8, 128)),
        y, flat_links, rate, znear, zfar,
    )
    zinner = swap(zinner, "src", True)
    next_tnear = swap(next_tnear, time, False)
    x, znear, zouter = stage(
        outer_kernel, (field, z_halos[0], shape(2, 12, 8, 128)),
        y, flat_links, rate, znear, zfar, tnear, both_tfar, inner_x, inner_near,
    )
    zouter = swap(zouter, "src", True)
    znear = swap(znear, "src", False)
    y = stage(local_kernel, field, x, src, flat_links, rate, scratch=carry)
    x = stage(last_kernel, flat, y, flat_links, rate, znear, zinner, zouter, next_tnear, both_tfar)
    return (guess.reshape(sources.shape), x.reshape(sources.shape))


def solution(mesh):
    return jax.shard_map(
        shards,
        mesh=mesh,
        in_specs=(
            P(None, None, ("lat", "sub"), "src", None),
            P(None, None, ("lat", "sub"), "src", None),
            P(),
            P(None, None, ("lat", "sub"), None, None),
            P("src"),
        ),
        out_specs=(
            P(None, None, ("lat", "sub"), "src", None),
            P(None, None, ("lat", "sub"), "src", None),
        ),
        check_vma=False,
    )
```

```python
import functools
import math

import jax
import jax.numpy as jnp
from jax import lax
from jax.experimental import pallas as pl
from jax.experimental.pallas import tpu as pltpu
from jax.sharding import PartitionSpec as P

LX = 16
HOPPING = 0.12

BLOCKS = [
    {(0, 1): 1, (1, 0): 1},
    {(0, 1): 2, (1, 0): 0},
    {(0, 0): 1, (1, 1): 3},
    {(0, 0): 0, (1, 1): 0},
]


def times_power(power, re, im):
    return [
        ((1, re), (1, im)),
        ((-1, im), (1, re)),
        ((-1, re), (-1, im)),
        ((1, im), (-1, re)),
    ][power % 4]


def add_signed(base, sign, value):
    return base + value if sign > 0 else base - value


def project(sign, direction, load):
    half = []
    for row in range(2):
        col, power = next((c, p) for (r, c), p in BLOCKS[direction].items() if r == row)
        colours = []
        for colour in range(3):
            lower_re, lower_im = load(0, 2 + col, colour), load(1, 2 + col, colour)
            (sr, vr), (si, vi) = times_power(power, lower_re, lower_im)
            colours.append(
                (
                    add_signed(load(0, row, colour), sr * sign, vr),
                    add_signed(load(1, row, colour), si * sign, vi),
                )
            )
        half.append(colours)
    return half


def rebuild_into(acc, sign, direction, half):
    def put(key, sgn, value):
        if key in acc:
            acc[key] = add_signed(acc[key], sgn, value)
        else:
            acc[key] = value if sgn > 0 else -value

    for row in range(2):
        for colour in range(3):
            re, im = half[row][colour]
            put((0, row, colour), 1, re)
            put((1, row, colour), 1, im)
    for (row, col), power in BLOCKS[direction].items():
        for colour in range(3):
            re, im = half[row][colour]
            (sr, vr), (si, vi) = times_power(-power, re, im)
            put((0, 2 + col, colour), sr * sign, vr)
            put((1, 2 + col, colour), si * sign, vi)


def colour_mul(link, half, adjoint):
    out = []
    for spin in range(2):
        rows = []
        for row in range(3):
            re = im = None
            for col in range(3):
                lr, li = link[(col, row)] if adjoint else link[(row, col)]
                hr, hi = half[spin][col]
                if adjoint:
                    tr, ti = lr * hr + li * hi, lr * hi - li * hr
                else:
                    tr, ti = lr * hr - li * hi, lr * hi + li * hr
                re = tr if re is None else re + tr
                im = ti if im is None else im + ti
            rows.append((re, im))
        out.append(rows)
    return out


def map_half(fn, half):
    return [[(fn(re), fn(im)) for re, im in rows] for rows in half]


def load_half(load):
    return [[(load(3 * s + c), load(6 + 3 * s + c)) for c in range(3)] for s in range(2)]


def store_half(store, half):
    for s in range(2):
        for c in range(3):
            store(3 * s + c, half[s][c][0])
            store(6 + 3 * s + c, half[s][c][1])


def load_link(links_ref, slices, direction, t):
    def one(comp):
        row = (direction * 18 + comp) * slices + t
        return jnp.broadcast_to(links_ref[pl.ds(row, 1), :], (8, 128))

    return {(a, c): (one(3 * a + c), one(9 + 3 * a + c)) for a in range(3) for c in range(3)}


def moved(direction, step):
    def fn(v):
        if direction == 1:
            return pltpu.roll(v, (-step * LX) % 128, 1)
        column = lax.rem(lax.broadcasted_iota(jnp.int32, v.shape, 1), LX)
        border = LX - 1 if step > 0 else 0
        inside = pltpu.roll(v, (-step) % 128, 1)
        wrapped = pltpu.roll(v, (step * (LX - 1)) % 128, 1)
        return jnp.where(column == border, wrapped, inside)

    return fn


def correlation_kernel(
    eig_hbm, src_hbm, links_hbm, damp_ref, out_ref, eig_ref, links_ref, src_ref, sems, *, nev, slices
):
    comps = 24
    sources = 8
    rows = sources * comps * slices // 2
    src_copies = [
        pltpu.make_async_copy(
            src_hbm.at[pl.ds(i * rows, rows)], src_ref.at[pl.ds(i * rows, rows)], sems.at[slices + i]
        )
        for i in range(2)
    ]
    eig_copies = [
        pltpu.make_async_copy(eig_hbm.at[:, t], eig_ref.at[:, t], sems.at[t]) for t in range(slices)
    ]
    links_copy = pltpu.make_async_copy(
        links_hbm.at[:, lax.axis_index("src")], links_ref, sems.at[slices + 2]
    )
    for copy in src_copies + eig_copies + [links_copy]:
        copy.start()
    for copy in src_copies:
        copy.wait()
    full = jnp.zeros((sources * comps, nev * comps), jnp.float32)
    for t in range(0, slices, 2):
        lhs = [
            src_ref[pl.ds(u, sources * comps, stride=slices), :].astype(jnp.bfloat16)
            for u in (t, t + 1)
        ]
        eig_copies[t].wait()
        eig_copies[t + 1].wait()
        rhs = [eig_ref[:, u].reshape(nev * comps, 128) for u in (t, t + 1)]
        full = full + lax.dot_general(
            jnp.concatenate(lhs, axis=1), jnp.concatenate(rhs, axis=1),
            (((1,), (1,)), ((), ())), preferred_element_type=jnp.float32,
        )
    row = lax.rem(lax.broadcasted_iota(jnp.int32, (sources * comps, 1), 0), comps)
    col = lax.rem(lax.broadcasted_iota(jnp.int32, (1, nev * comps), 1), comps)
    gap = row - col
    straight = jnp.where(gap == 0, full, 0.0)
    crossed = jnp.where(gap == 12, full, 0.0) - jnp.where(gap == -12, full, 0.0)
    straight = straight.reshape(sources, comps, nev * comps).sum(1)
    crossed = crossed.reshape(sources, comps, nev * comps).sum(1)
    both = jnp.concatenate([straight, crossed], axis=0)
    high = both.astype(jnp.bfloat16)
    middle = (both - high.astype(jnp.float32)).astype(jnp.bfloat16)
    low = (both - high.astype(jnp.float32) - middle.astype(jnp.float32)).astype(jnp.bfloat16)
    parts = jnp.concatenate([high, middle, low], axis=0)
    first = lax.broadcasted_iota(jnp.int32, (nev * comps, 128), 0)
    start = lax.broadcasted_iota(jnp.int32, (nev * comps, 128), 1) * comps
    gather = jnp.where((first >= start) & (first < start + comps), 1.0, 0.0).astype(jnp.bfloat16)
    sums = jnp.dot(parts, gather, preferred_element_type=jnp.float32)
    sums = (sums[0:16] + sums[16:32]) + sums[32:48]
    total = sums[0:8] + pltpu.roll(sums[8:16], nev, 1)
    links_copy.wait()
    holder = (lax.axis_index("lat") == 0) & (lax.axis_index("sub") == 0)
    value = jnp.where(holder, damp_ref[0], 0.0)
    at_row = lax.broadcasted_iota(jnp.int32, (8, 128), 0) == lax.axis_index("src")
    at_lane = lax.broadcasted_iota(jnp.int32, (8, 128), 1) == 2 * nev
    total = total + jnp.where(at_row & at_lane, value, 0.0)
    out_ref[...] = jnp.broadcast_to(total[None], out_ref.shape)


def choose(flag, half_true, half_false):
    return [
        [
            tuple(jnp.where(flag, a, b) for a, b in zip(half_true[s][c], half_false[s][c]))
            for c in range(3)
        ]
        for s in range(2)
    ]


def z_even():
    return lax.rem(lax.axis_index("src"), 2) == 0


def t_place():
    place = lax.axis_index(("lat", "sub"))
    return place, lax.rem(place, 2) == 0


def emit_halos(load, links_ref, t, near_ref, far_ref, slices, near_t=None, far_t=None):
    even = z_even()
    up = project(1, 2, load)
    up = colour_mul(load_link(links_ref, slices, 2, t), up, True)
    down = project(-1, 2, load)
    near_t, far_t = (t if place is None else place for place in (near_t, far_t))
    store_half(lambda i, v: near_ref.__setitem__((near_t, i), v), choose(even, up, down))
    store_half(lambda i, v: far_ref.__setitem__((far_t, i), v), choose(even, down, up))


def emit_time_halos(load_last, load_first, links_ref, near_ref, far_ref, slices):
    place, even = t_place()
    extent = lax.axis_size(("lat", "sub"))
    up_sign = jnp.where(place == extent - 1, -1.0, 1.0)
    down_sign = jnp.where(place == 0, -1.0, 1.0)
    last = slices - 1
    up = project(1, 3, load_last)
    up = colour_mul(load_link(links_ref, slices, 3, last), up, True)
    up = map_half(lambda v: v * up_sign, up)
    down = project(-1, 3, load_first)
    down = map_half(lambda v: v * down_sign, down)
    store_half(lambda i, v: near_ref.__setitem__(i, v), choose(even, up, down))
    store_half(lambda i, v: far_ref.__setitem__(i, v), choose(even, down, up))


def guess_kernel(
    part_ref, ev_ref, eig_ref, links_ref,
    x_ref, rate_ref, guess_ref, znear_ref, zfar_ref, tnear_ref, tfar_ref,
    *, nev, slices, norm,
):
    comps = 24
    total = part_ref[0]
    for i in range(1, part_ref.shape[0]):
        total = total + part_ref[i]
    ev = ev_ref[...]
    w_re = ((total[:, :nev] / norm) / ev).astype(jnp.bfloat16)
    w_im = ((total[:, nev : 2 * nev] / norm) / ev).astype(jnp.bfloat16)
    rate_ref[...] = jnp.broadcast_to(total[:, 2 * nev : 2 * nev + 1], (8, 128))
    row = lax.broadcasted_iota(jnp.int32, (nev, nev * comps), 0) * comps
    col = lax.broadcasted_iota(jnp.int32, (nev, nev * comps), 1)
    spread = jnp.where((col >= row) & (col < row + comps), 1.0, 0.0).astype(jnp.bfloat16)
    w_re = jnp.dot(w_re, spread, preferred_element_type=jnp.float32)
    w_im = jnp.dot(w_im, spread, preferred_element_type=jnp.float32)
    comp = lax.rem(lax.broadcasted_iota(jnp.int32, (8, nev * comps), 1), comps)
    blocks = []
    for c in range(comps):
        other, turned = (c + 12, -w_im) if c < 12 else (c - 12, w_im)
        blocks.append(jnp.where(comp == c, w_re, jnp.where(comp == other, turned, 0.0)))
    mix = jnp.concatenate(blocks, axis=0).astype(jnp.bfloat16)
    for t in range(slices):
        res = jnp.dot(
            mix, eig_ref[:, t].reshape(nev * comps, 128), preferred_element_type=jnp.float32
        )
        x_ref[t] = res.reshape(comps, 8, 128)

    def step(t, carry):
        for c in range(comps):
            guess_ref[pl.ds(c * slices + t, 8, stride=comps * slices), :] = x_ref[t, c]
        emit_halos(
            lambda p, s, c: x_ref[t, 12 * p + 3 * s + c],
            links_ref, t, znear_ref, zfar_ref, slices,
        )
        return carry

    lax.fori_loop(0, slices, step, 0)
    load = lambda t: lambda p, s, c: x_ref[t, 12 * p + 3 * s + c]
    emit_time_halos(load(slices - 1), load(0), links_ref, tnear_ref, tfar_ref, slices)


def copies_out(src_ref, dst_ref, sems):
    rows = src_ref.shape[0] // 8
    return [
        pltpu.make_async_copy(
            src_ref.at[pl.ds(i * rows, rows)], dst_ref.at[pl.ds(i * rows, rows)], sems.at[i]
        )
        for i in range(8)
    ]


def local_and_copy_kernel(
    x_ref, src_ref, links_ref, rate_ref, held_ref, y_ref, out_hbm, behind_ref, sems, *, slices
):
    copies = copies_out(held_ref, out_hbm, sems)
    for copy in copies:
        copy.start()
    local_kernel(x_ref, src_ref, links_ref, rate_ref, y_ref, behind_ref, slices=slices)
    for copy in copies:
        copy.wait()


def local_kernel(x_ref, src_ref, links_ref, rate_ref, y_ref, behind_ref, *, slices):
    behind_ref[...] = jnp.zeros_like(behind_ref)

    def step(t, carry):
        load = lambda p, s, c: x_ref[t, 12 * p + 3 * s + c]
        acc = {}
        for direction in range(2):
            link = load_link(links_ref, slices, direction, t)
            ahead = map_half(moved(direction, 1), project(-1, direction, load))
            rebuild_into(acc, -1, direction, colour_mul(link, ahead, False))
            behind = colour_mul(link, project(1, direction, load), True)
            rebuild_into(acc, 1, direction, map_half(moved(direction, -1), behind))
        link = load_link(links_ref, slices, 3, t)
        inside = jnp.where(t == slices - 1, 0.0, 1.0)
        following = jnp.minimum(t + 1, slices - 1)
        ahead = project(-1, 3, lambda p, s, c: x_ref[following, 12 * p + 3 * s + c])
        ahead = map_half(lambda v: v * inside, ahead)
        rebuild_into(acc, -1, 3, colour_mul(link, ahead, False))
        rebuild_into(acc, 1, 3, load_half(lambda i: behind_ref[i]))
        up = colour_mul(link, project(1, 3, load), True)
        store_half(lambda i, v: behind_ref.__setitem__(i, v), up)
        rate = rate_ref[...]
        for (p, s, c), hop in acc.items():
            comp = 12 * p + 3 * s + c
            where = pl.ds(comp * slices + t, 8, stride=24 * slices)
            value = load(p, s, c)
            y_ref[t, comp] = value + rate * (src_ref[where, :] - (value - HOPPING * hop))
        return carry

    lax.fori_loop(0, slices, step, 0)


def z_hops(links_ref, znear_ref, zfar_ref, t, slices, far_t=None):
    above_near = z_even()
    acc = {}
    far_t = t if far_t is None else far_t
    near = load_half(lambda i: znear_ref[t, i])
    far = load_half(lambda i: zfar_ref[far_t, i])
    link = load_link(links_ref, slices, 2, t)
    rebuild_into(acc, -1, 2, colour_mul(link, choose(above_near, near, far), False))
    rebuild_into(acc, 1, 2, choose(above_near, far, near))
    return acc


def edge_kernel(
    y_ref, links_ref, rate_ref, znear_ref, zfar_ref, first_ref, tnear_ref, tfar_ref, *, slices
):
    rate = rate_ref[...] * HOPPING

    def load(t):
        hops = z_hops(links_ref, znear_ref, zfar_ref, t, slices)
        return lambda p, s, c: y_ref[t, 12 * p + 3 * s + c] + rate * hops[(p, s, c)]

    tfar_ref[0] = first_ref[...]
    emit_time_halos(load(slices - 1), load(0), links_ref, tnear_ref, tfar_ref.at[1], slices)


def inner_kernel(
    y_ref, links_ref, rate_ref, znear_ref, zfar_ref, x_ref, near_ref, far_ref, *, slices
):
    def step(t, carry):
        rate = rate_ref[...] * HOPPING
        new = {}
        for (p, s, c), hop in z_hops(links_ref, znear_ref, zfar_ref, t, slices).items():
            comp = 12 * p + 3 * s + c
            new[(p, s, c)] = y_ref[t, comp] + rate * hop
            x_ref[t - 1, comp] = new[(p, s, c)]
        emit_halos(
            lambda p, s, c: new[(p, s, c)], links_ref, t, near_ref, far_ref, slices, t - 1, t - 1
        )
        return carry

    lax.fori_loop(1, slices - 1, step, 0)


def t_hops(links_ref, tnear_ref, tfar_ref, slices):
    _, even = t_place()
    near, far = (load_half(lambda i, ref=ref: ref[i]) for ref in (tnear_ref, tfar_ref))
    first, last = {}, {}
    rebuild_into(first, 1, 3, choose(even, far, near))
    link = load_link(links_ref, slices, 3, slices - 1)
    rebuild_into(last, -1, 3, colour_mul(link, choose(even, near, far), False))
    return first, last


def outer_kernel(
    y_ref, links_ref, rate_ref, znear_ref, zfar_ref, tnear_ref, tfar_ref, inner_x_ref, inner_near_ref,
    x_ref, near_ref, far_ref, *, slices,
):
    x_ref[1 : slices - 1] = inner_x_ref[...]
    near_ref[1 : slices - 1] = inner_near_ref[...]
    rate = rate_ref[...] * HOPPING
    for i, hops in enumerate(t_hops(links_ref, tnear_ref, tfar_ref.at[0], slices)):
        t = (slices - 1) * i
        new = {}
        for (p, s, c), hop in z_hops(links_ref, znear_ref, zfar_ref, t, slices).items():
            comp = 12 * p + 3 * s + c
            new[(p, s, c)] = y_ref[t, comp] + rate * (hop + hops[(p, s, c)])
            x_ref[t, comp] = new[(p, s, c)]
        emit_halos(
            lambda p, s, c: new[(p, s, c)], links_ref, t, near_ref, far_ref, slices, t, i
        )


def last_kernel(
    y_ref, links_ref, rate_ref, znear_ref, zinner_ref, zouter_ref, tnear_ref, tfar_ref,
    out_hbm, out_ref, sems, *, slices,
):
    rate = rate_ref[...] * HOPPING

    def finish(t, hops, more=None):
        for key, hop in hops.items():
            p, s, c = key
            comp = 12 * p + 3 * s + c
            hop = hop if more is None else hop + more[key]
            where = pl.ds(comp * slices + t, 8, stride=24 * slices)
            out_ref[where, :] = y_ref[t, comp] + rate * hop

    for i, more in enumerate(t_hops(links_ref, tnear_ref, tfar_ref.at[1], slices)):
        t = (slices - 1) * i
        finish(t, z_hops(links_ref, znear_ref, zouter_ref, t, slices, i), more)

    def step(t, carry):
        finish(t, z_hops(links_ref, znear_ref, zinner_ref, t, slices, t - 1))
        return carry

    lax.fori_loop(1, slices - 1, step, 0)
    copies = copies_out(out_ref, out_hbm, sems)
    for copy in copies:
        copy.start()
    for copy in copies:
        copy.wait()


def call(kernel, outs, ins, flops, hbm=(), smem=(), scratch=(), hbm_outs=()):
    space = lambda i: pltpu.HBM if i in hbm else pltpu.SMEM if i in smem else pltpu.VMEM
    out_space = lambda i: pltpu.HBM if i in hbm_outs else pltpu.VMEM
    single = not isinstance(outs, tuple)
    return pl.pallas_call(
        kernel,
        out_shape=outs,
        in_specs=[pl.BlockSpec(memory_space=space(i)) for i in range(ins)],
        out_specs=pl.BlockSpec(memory_space=out_space(0))
        if single
        else tuple(pl.BlockSpec(memory_space=out_space(i)) for i in range(len(outs))),
        scratch_shapes=list(scratch),
        compiler_params=pltpu.CompilerParams(vmem_limit_bytes=24 << 20),
        cost_estimate=pl.CostEstimate(
            flops=flops, bytes_accessed=3_000_000, transcendentals=0
        ),
    )


def swap(x, axis, far):
    n = lax.axis_size(axis)
    partner = lambda i: (i + 1 if i % 2 else i - 1) % n if far else i ^ 1
    return lax.ppermute(x, axis, [(i, partner(i)) for i in range(n)])


def shards(sources, eigvecs, eigvals, links, damping):
    count, comps, slices = sources.shape[:3]
    nev = eigvecs.shape[0]
    zdim = links.shape[3]
    devices = lax.axis_size(("src", "lat", "sub"))
    norm = math.sqrt(comps * slices * 128 * devices)
    f32 = jnp.float32

    src = sources.reshape(count * comps * slices, 128)
    eig = eigvecs.transpose(0, 2, 3, 1, 4).reshape(nev, slices, comps, 128)

    shape = lambda *dims: jax.ShapeDtypeStruct(dims, f32)
    lat, rest = lax.axis_size("lat"), lax.axis_size(("sub", "src"))
    hbm = lambda x: pltpu.with_memory_space_constraint(x, pltpu.HBM)
    slab = shape(4 * 18 * slices, 128)
    partial, eig, flat_links = call(
        functools.partial(correlation_kernel, nev=nev, slices=slices),
        (shape(lat, 8, 128), jax.ShapeDtypeStruct(eig.shape, eig.dtype), slab),
        4, 226_000_000, hbm=(0, 1, 2), smem=(3,),
        scratch=[
            pltpu.VMEM(src.shape, f32),
            pltpu.SemaphoreType.DMA((slices + 3,)),
        ],
    )(hbm(eig), hbm(src), hbm(links.reshape(4 * 18 * slices, zdim, 128)), damping)
    partial = lax.all_to_all(partial, "lat", 0, 0, tiled=True)
    partial = jnp.broadcast_to(partial.sum(0)[None], (rest, 8, 128))
    partial = lax.all_to_all(partial, ("sub", "src"), 0, 0, tiled=True)

    field = shape(slices, comps, 8, 128)
    z_halos = (shape(slices, 12, 8, 128),) * 2
    t_halos = (shape(12, 8, 128),) * 2
    flat = shape(count * comps * slices, 128)
    x, rate, guess, znear, zfar, tnear, tfar = call(
        functools.partial(guess_kernel, nev=nev, slices=slices, norm=norm),
        (field, shape(8, 128), pltpu.VMEM(flat.shape, f32)) + z_halos + t_halos,
        4, 226_000_000,
    )(partial, eigvals.reshape(1, nev), eig, flat_links)

    time = ("lat", "sub")

    def stage(kernel, outs, *args, scratch=(), hbm_outs=()):
        return call(
            functools.partial(kernel, slices=slices), outs, len(args),
            5_000_000, scratch=scratch, hbm_outs=hbm_outs,
        )(*args)

    carry = [pltpu.VMEM((12, 8, 128), f32)]
    zfar = swap(zfar, "src", True)
    znear = swap(znear, "src", False)
    tnear = swap(tnear, time, False)
    y = stage(local_kernel, field, x, src, flat_links, rate, scratch=carry)
    next_tnear, both_tfar = stage(
        edge_kernel, (shape(12, 8, 128), shape(2, 12, 8, 128)),
        y, flat_links, rate, znear, zfar, tfar,
    )
    both_tfar = swap(both_tfar, time, True)
    inner = slices - 2
    inner_x, inner_near, zinner = stage(
        inner_kernel,
        (shape(inner, comps, 8, 128), shape(inner, 12, 8, 128), shape(inner, 12, 8, 128)),
        y, flat_links, rate, znear, zfar,
    )
    zinner = swap(zinner, "src", True)
    next_tnear = swap(next_tnear, time, False)
    x, znear, zouter = stage(
        outer_kernel, (field, z_halos[0], shape(2, 12, 8, 128)),
        y, flat_links, rate, znear, zfar, tnear, both_tfar, inner_x, inner_near,
    )
    zouter = swap(zouter, "src", True)
    znear = swap(znear, "src", False)
    y, guess = stage(
        local_and_copy_kernel, (field, flat), x, src, flat_links, rate, guess,
        scratch=carry + [pltpu.SemaphoreType.DMA((8,))], hbm_outs=(1,),
    )
    x = stage(
        last_kernel, flat, y, flat_links, rate, znear, zinner, zouter, next_tnear, both_tfar,
        scratch=[pltpu.VMEM(flat.shape, f32), pltpu.SemaphoreType.DMA((8,))], hbm_outs=(0,),
    )
    return (guess.reshape(sources.shape), x.reshape(sources.shape))


def solution(mesh):
    return jax.shard_map(
        shards,
        mesh=mesh,
        in_specs=(
            P(None, None, ("lat", "sub"), "src", None),
            P(None, None, ("lat", "sub"), "src", None),
            P(),
            P(None, None, ("lat", "sub"), None, None),
            P("src"),
        ),
        out_specs=(
            P(None, None, ("lat", "sub"), "src", None),
            P(None, None, ("lat", "sub"), "src", None),
        ),
        check_vma=False,
    )
```

```python
import functools
import math

import jax
import jax.numpy as jnp
from jax import lax
from jax.experimental import pallas as pl
from jax.experimental.pallas import tpu as pltpu
from jax.sharding import PartitionSpec as P

LX = 16
HOPPING = 0.12

BLOCKS = [
    {(0, 1): 1, (1, 0): 1},
    {(0, 1): 2, (1, 0): 0},
    {(0, 0): 1, (1, 1): 3},
    {(0, 0): 0, (1, 1): 0},
]


def times_power(power, re, im):
    return [
        ((1, re), (1, im)),
        ((-1, im), (1, re)),
        ((-1, re), (-1, im)),
        ((1, im), (-1, re)),
    ][power % 4]


def add_signed(base, sign, value):
    return base + value if sign > 0 else base - value


def project(sign, direction, load):
    half = []
    for row in range(2):
        col, power = next((c, p) for (r, c), p in BLOCKS[direction].items() if r == row)
        colours = []
        for colour in range(3):
            lower_re, lower_im = load(0, 2 + col, colour), load(1, 2 + col, colour)
            (sr, vr), (si, vi) = times_power(power, lower_re, lower_im)
            colours.append(
                (
                    add_signed(load(0, row, colour), sr * sign, vr),
                    add_signed(load(1, row, colour), si * sign, vi),
                )
            )
        half.append(colours)
    return half


def rebuild_into(acc, sign, direction, half):
    def put(key, sgn, value):
        if key in acc:
            acc[key] = add_signed(acc[key], sgn, value)
        else:
            acc[key] = value if sgn > 0 else -value

    for row in range(2):
        for colour in range(3):
            re, im = half[row][colour]
            put((0, row, colour), 1, re)
            put((1, row, colour), 1, im)
    for (row, col), power in BLOCKS[direction].items():
        for colour in range(3):
            re, im = half[row][colour]
            (sr, vr), (si, vi) = times_power(-power, re, im)
            put((0, 2 + col, colour), sr * sign, vr)
            put((1, 2 + col, colour), si * sign, vi)


def colour_mul(link, half, adjoint):
    out = []
    for spin in range(2):
        rows = []
        for row in range(3):
            re = im = None
            for col in range(3):
                lr, li = link[(col, row)] if adjoint else link[(row, col)]
                hr, hi = half[spin][col]
                if adjoint:
                    tr, ti = lr * hr + li * hi, lr * hi - li * hr
                else:
                    tr, ti = lr * hr - li * hi, lr * hi + li * hr
                re = tr if re is None else re + tr
                im = ti if im is None else im + ti
            rows.append((re, im))
        out.append(rows)
    return out


def map_half(fn, half):
    return [[(fn(re), fn(im)) for re, im in rows] for rows in half]


def load_half(load):
    return [[(load(3 * s + c), load(6 + 3 * s + c)) for c in range(3)] for s in range(2)]


def store_half(store, half):
    for s in range(2):
        for c in range(3):
            store(3 * s + c, half[s][c][0])
            store(6 + 3 * s + c, half[s][c][1])


def load_link(links_ref, slices, direction, t):
    def one(comp):
        row = (direction * 18 + comp) * slices + t
        return jnp.broadcast_to(links_ref[pl.ds(row, 1), :], (8, 128))

    return {(a, c): (one(3 * a + c), one(9 + 3 * a + c)) for a in range(3) for c in range(3)}


def moved(direction, step):
    def fn(v):
        if direction == 1:
            return pltpu.roll(v, (-step * LX) % 128, 1)
        column = lax.rem(lax.broadcasted_iota(jnp.int32, v.shape, 1), LX)
        border = LX - 1 if step > 0 else 0
        inside = pltpu.roll(v, (-step) % 128, 1)
        wrapped = pltpu.roll(v, (step * (LX - 1)) % 128, 1)
        return jnp.where(column == border, wrapped, inside)

    return fn


def correlation_kernel(
    eig_hbm, src_hbm, links_hbm, damp_ref, out_ref, eig_ref, links_ref, src_ref, sems, *, nev, slices
):
    comps = 24
    sources = 8
    rows = sources * comps * slices // 2
    src_copies = [
        pltpu.make_async_copy(
            src_hbm.at[pl.ds(i * rows, rows)], src_ref.at[pl.ds(i * rows, rows)], sems.at[slices + i]
        )
        for i in range(2)
    ]
    eig_copies = [
        pltpu.make_async_copy(eig_hbm.at[:, t], eig_ref.at[:, t], sems.at[t]) for t in range(slices)
    ]
    links_copy = pltpu.make_async_copy(
        links_hbm.at[:, lax.axis_index("src")], links_ref, sems.at[slices + 2]
    )
    for copy in src_copies + eig_copies + [links_copy]:
        copy.start()
    for copy in src_copies:
        copy.wait()
    row = lax.rem(lax.broadcasted_iota(jnp.int32, (sources * comps, 1), 0), comps)
    col = lax.rem(lax.broadcasted_iota(jnp.int32, (1, nev * comps), 1), comps)
    gap = row - col
    first = lax.broadcasted_iota(jnp.int32, (nev * comps, 128), 0)
    start = lax.broadcasted_iota(jnp.int32, (nev * comps, 128), 1) * comps
    gather = jnp.where((first >= start) & (first < start + comps), 1.0, 0.0).astype(jnp.bfloat16)
    lhs = [
        src_ref[pl.ds(t, sources * comps, stride=slices), :].astype(jnp.bfloat16)
        for t in range(slices)
    ]
    full = jnp.zeros((sources * comps, nev * comps), jnp.float32)
    for t in range(0, slices, 2):
        eig_copies[t].wait()
        eig_copies[t + 1].wait()
        rhs = [eig_ref[:, u].reshape(nev * comps, 128) for u in (t, t + 1)]
        full = full + lax.dot_general(
            jnp.concatenate(lhs[t : t + 2], axis=1), jnp.concatenate(rhs, axis=1),
            (((1,), (1,)), ((), ())), preferred_element_type=jnp.float32,
        )
    straight = jnp.where(gap == 0, full, 0.0)
    crossed = jnp.where(gap == 12, full, 0.0) - jnp.where(gap == -12, full, 0.0)
    straight = straight.reshape(sources, comps, nev * comps).sum(1)
    crossed = crossed.reshape(sources, comps, nev * comps).sum(1)
    both = jnp.concatenate([straight, crossed], axis=0)
    high = both.astype(jnp.bfloat16)
    middle = (both - high.astype(jnp.float32)).astype(jnp.bfloat16)
    low = (both - high.astype(jnp.float32) - middle.astype(jnp.float32)).astype(jnp.bfloat16)
    parts = jnp.concatenate([high, middle, low], axis=0)
    sums = jnp.dot(parts, gather, preferred_element_type=jnp.float32)
    sums = (sums[0:16] + sums[16:32]) + sums[32:48]
    total = sums[0:8] + pltpu.roll(sums[8:16], nev, 1)
    links_copy.wait()
    holder = (lax.axis_index("lat") == 0) & (lax.axis_index("sub") == 0)
    value = jnp.where(holder, damp_ref[0], 0.0)
    at_row = lax.broadcasted_iota(jnp.int32, (8, 128), 0) == lax.axis_index("src")
    at_lane = lax.broadcasted_iota(jnp.int32, (8, 128), 1) == 2 * nev
    total = total + jnp.where(at_row & at_lane, value, 0.0)
    out_ref[...] = jnp.broadcast_to(total[None], out_ref.shape)


def choose(flag, half_true, half_false):
    return [
        [
            tuple(jnp.where(flag, a, b) for a, b in zip(half_true[s][c], half_false[s][c]))
            for c in range(3)
        ]
        for s in range(2)
    ]


def z_even():
    return lax.rem(lax.axis_index("src"), 2) == 0


def t_place():
    place = lax.axis_index(("lat", "sub"))
    return place, lax.rem(place, 2) == 0


def emit_halos(load, links_ref, t, near_ref, far_ref, slices, near_t=None, far_t=None):
    even = z_even()
    up = project(1, 2, load)
    up = colour_mul(load_link(links_ref, slices, 2, t), up, True)
    down = project(-1, 2, load)
    near_t, far_t = (t if place is None else place for place in (near_t, far_t))
    store_half(lambda i, v: near_ref.__setitem__((near_t, i), v), choose(even, up, down))
    store_half(lambda i, v: far_ref.__setitem__((far_t, i), v), choose(even, down, up))


def emit_time_halos(load_last, load_first, links_ref, near_ref, far_ref, slices):
    place, even = t_place()
    extent = lax.axis_size(("lat", "sub"))
    up_sign = jnp.where(place == extent - 1, -1.0, 1.0)
    down_sign = jnp.where(place == 0, -1.0, 1.0)
    last = slices - 1
    up = project(1, 3, load_last)
    up = colour_mul(load_link(links_ref, slices, 3, last), up, True)
    up = map_half(lambda v: v * up_sign, up)
    down = project(-1, 3, load_first)
    down = map_half(lambda v: v * down_sign, down)
    store_half(lambda i, v: near_ref.__setitem__(i, v), choose(even, up, down))
    store_half(lambda i, v: far_ref.__setitem__(i, v), choose(even, down, up))


def guess_kernel(
    part_ref, ev_ref, eig_ref, links_ref,
    x_ref, rate_ref, guess_ref, znear_ref, zfar_ref, tnear_ref, tfar_ref,
    *, nev, slices, norm,
):
    comps = 24
    total = part_ref[0]
    for i in range(1, part_ref.shape[0]):
        total = total + part_ref[i]
    ev = ev_ref[...]
    w_re = ((total[:, :nev] / norm) / ev).astype(jnp.bfloat16)
    w_im = ((total[:, nev : 2 * nev] / norm) / ev).astype(jnp.bfloat16)
    rate_ref[...] = jnp.broadcast_to(total[:, 2 * nev : 2 * nev + 1], (8, 128))
    row = lax.broadcasted_iota(jnp.int32, (nev, nev * comps), 0) * comps
    col = lax.broadcasted_iota(jnp.int32, (nev, nev * comps), 1)
    spread = jnp.where((col >= row) & (col < row + comps), 1.0, 0.0).astype(jnp.bfloat16)
    w_re = jnp.dot(w_re, spread, preferred_element_type=jnp.float32)
    w_im = jnp.dot(w_im, spread, preferred_element_type=jnp.float32)
    comp = lax.rem(lax.broadcasted_iota(jnp.int32, (8, nev * comps), 1), comps)
    blocks = []
    for c in range(comps):
        other, turned = (c + 12, -w_im) if c < 12 else (c - 12, w_im)
        blocks.append(jnp.where(comp == c, w_re, jnp.where(comp == other, turned, 0.0)))
    mix = jnp.concatenate(blocks, axis=0).astype(jnp.bfloat16)
    for t in range(slices):
        res = jnp.dot(
            mix, eig_ref[:, t].reshape(nev * comps, 128), preferred_element_type=jnp.float32
        )
        x_ref[t] = res.reshape(comps, 8, 128)

    def step(t, carry):
        for c in range(comps):
            guess_ref[pl.ds(c * slices + t, 8, stride=comps * slices), :] = x_ref[t, c]
        emit_halos(
            lambda p, s, c: x_ref[t, 12 * p + 3 * s + c],
            links_ref, t, znear_ref, zfar_ref, slices,
        )
        return carry

    lax.fori_loop(0, slices, step, 0)
    load = lambda t: lambda p, s, c: x_ref[t, 12 * p + 3 * s + c]
    emit_time_halos(load(slices - 1), load(0), links_ref, tnear_ref, tfar_ref, slices)


def copies_out(src_ref, dst_ref, sems):
    rows = src_ref.shape[0] // 8
    return [
        pltpu.make_async_copy(
            src_ref.at[pl.ds(i * rows, rows)], dst_ref.at[pl.ds(i * rows, rows)], sems.at[i]
        )
        for i in range(8)
    ]


def local_and_copy_kernel(
    x_ref, src_ref, links_ref, rate_ref, held_ref, y_ref, out_hbm, behind_ref, sems, *, slices
):
    copies = copies_out(held_ref, out_hbm, sems)
    for copy in copies:
        copy.start()
    local_kernel(x_ref, src_ref, links_ref, rate_ref, y_ref, behind_ref, slices=slices)
    for copy in copies:
        copy.wait()


def local_kernel(x_ref, src_ref, links_ref, rate_ref, y_ref, behind_ref, *, slices):
    behind_ref[...] = jnp.zeros_like(behind_ref)

    def step(t, carry):
        load = lambda p, s, c: x_ref[t, 12 * p + 3 * s + c]
        acc = {}
        for direction in range(2):
            link = load_link(links_ref, slices, direction, t)
            ahead = map_half(moved(direction, 1), project(-1, direction, load))
            rebuild_into(acc, -1, direction, colour_mul(link, ahead, False))
            behind = colour_mul(link, project(1, direction, load), True)
            rebuild_into(acc, 1, direction, map_half(moved(direction, -1), behind))
        link = load_link(links_ref, slices, 3, t)
        inside = jnp.where(t == slices - 1, 0.0, 1.0)
        following = jnp.minimum(t + 1, slices - 1)
        ahead = project(-1, 3, lambda p, s, c: x_ref[following, 12 * p + 3 * s + c])
        ahead = map_half(lambda v: v * inside, ahead)
        rebuild_into(acc, -1, 3, colour_mul(link, ahead, False))
        rebuild_into(acc, 1, 3, load_half(lambda i: behind_ref[i]))
        up = colour_mul(link, project(1, 3, load), True)
        store_half(lambda i, v: behind_ref.__setitem__(i, v), up)
        rate = rate_ref[...]
        for (p, s, c), hop in acc.items():
            comp = 12 * p + 3 * s + c
            where = pl.ds(comp * slices + t, 8, stride=24 * slices)
            value = load(p, s, c)
            y_ref[t, comp] = value + rate * (src_ref[where, :] - (value - HOPPING * hop))
        return carry

    lax.fori_loop(0, slices, step, 0)


def z_hops(links_ref, znear_ref, zfar_ref, t, slices, far_t=None):
    above_near = z_even()
    acc = {}
    far_t = t if far_t is None else far_t
    near = load_half(lambda i: znear_ref[t, i])
    far = load_half(lambda i: zfar_ref[far_t, i])
    link = load_link(links_ref, slices, 2, t)
    rebuild_into(acc, -1, 2, colour_mul(link, choose(above_near, near, far), False))
    rebuild_into(acc, 1, 2, choose(above_near, far, near))
    return acc


def edge_kernel(
    y_ref, links_ref, rate_ref, znear_ref, zfar_ref, first_ref, tnear_ref, tfar_ref, *, slices
):
    rate = rate_ref[...] * HOPPING

    def load(t):
        hops = z_hops(links_ref, znear_ref, zfar_ref, t, slices)
        return lambda p, s, c: y_ref[t, 12 * p + 3 * s + c] + rate * hops[(p, s, c)]

    tfar_ref[0] = first_ref[...]
    emit_time_halos(load(slices - 1), load(0), links_ref, tnear_ref, tfar_ref.at[1], slices)


def inner_kernel(
    y_ref, links_ref, rate_ref, znear_ref, zfar_ref, x_ref, near_ref, far_ref, *, slices
):
    def step(t, carry):
        rate = rate_ref[...] * HOPPING
        new = {}
        for (p, s, c), hop in z_hops(links_ref, znear_ref, zfar_ref, t, slices).items():
            comp = 12 * p + 3 * s + c
            new[(p, s, c)] = y_ref[t, comp] + rate * hop
            x_ref[t - 1, comp] = new[(p, s, c)]
        emit_halos(
            lambda p, s, c: new[(p, s, c)], links_ref, t, near_ref, far_ref, slices, t - 1, t - 1
        )
        return carry

    lax.fori_loop(1, slices - 1, step, 0)


def t_hops(links_ref, tnear_ref, tfar_ref, slices):
    _, even = t_place()
    near, far = (load_half(lambda i, ref=ref: ref[i]) for ref in (tnear_ref, tfar_ref))
    first, last = {}, {}
    rebuild_into(first, 1, 3, choose(even, far, near))
    link = load_link(links_ref, slices, 3, slices - 1)
    rebuild_into(last, -1, 3, colour_mul(link, choose(even, near, far), False))
    return first, last


def outer_kernel(
    y_ref, links_ref, rate_ref, znear_ref, zfar_ref, tnear_ref, tfar_ref, inner_x_ref, inner_near_ref,
    x_ref, near_ref, far_ref, *, slices,
):
    x_ref[1 : slices - 1] = inner_x_ref[...]
    near_ref[1 : slices - 1] = inner_near_ref[...]
    rate = rate_ref[...] * HOPPING
    for i, hops in enumerate(t_hops(links_ref, tnear_ref, tfar_ref.at[0], slices)):
        t = (slices - 1) * i
        new = {}
        for (p, s, c), hop in z_hops(links_ref, znear_ref, zfar_ref, t, slices).items():
            comp = 12 * p + 3 * s + c
            new[(p, s, c)] = y_ref[t, comp] + rate * (hop + hops[(p, s, c)])
            x_ref[t, comp] = new[(p, s, c)]
        emit_halos(
            lambda p, s, c: new[(p, s, c)], links_ref, t, near_ref, far_ref, slices, t, i
        )


def last_kernel(
    y_ref, links_ref, rate_ref, znear_ref, zinner_ref, zouter_ref, tnear_ref, tfar_ref,
    out_hbm, out_ref, sems, *, slices,
):
    rate = rate_ref[...] * HOPPING

    def finish(t, hops, more=None):
        for key, hop in hops.items():
            p, s, c = key
            comp = 12 * p + 3 * s + c
            hop = hop if more is None else hop + more[key]
            where = pl.ds(comp * slices + t, 8, stride=24 * slices)
            out_ref[where, :] = y_ref[t, comp] + rate * hop

    for i, more in enumerate(t_hops(links_ref, tnear_ref, tfar_ref.at[1], slices)):
        t = (slices - 1) * i
        finish(t, z_hops(links_ref, znear_ref, zouter_ref, t, slices, i), more)

    def step(t, carry):
        finish(t, z_hops(links_ref, znear_ref, zinner_ref, t, slices, t - 1))
        return carry

    lax.fori_loop(1, slices - 1, step, 0)
    copies = copies_out(out_ref, out_hbm, sems)
    for copy in copies:
        copy.start()
    for copy in copies:
        copy.wait()


def call(kernel, outs, ins, flops, hbm=(), smem=(), scratch=(), hbm_outs=()):
    space = lambda i: pltpu.HBM if i in hbm else pltpu.SMEM if i in smem else pltpu.VMEM
    out_space = lambda i: pltpu.HBM if i in hbm_outs else pltpu.VMEM
    single = not isinstance(outs, tuple)
    return pl.pallas_call(
        kernel,
        out_shape=outs,
        in_specs=[pl.BlockSpec(memory_space=space(i)) for i in range(ins)],
        out_specs=pl.BlockSpec(memory_space=out_space(0))
        if single
        else tuple(pl.BlockSpec(memory_space=out_space(i)) for i in range(len(outs))),
        scratch_shapes=list(scratch),
        compiler_params=pltpu.CompilerParams(vmem_limit_bytes=24 << 20),
        cost_estimate=pl.CostEstimate(
            flops=flops, bytes_accessed=3_000_000, transcendentals=0
        ),
    )


def swap(x, axis, far):
    n = lax.axis_size(axis)
    partner = lambda i: (i + 1 if i % 2 else i - 1) % n if far else i ^ 1
    return lax.ppermute(x, axis, [(i, partner(i)) for i in range(n)])


def shards(sources, eigvecs, eigvals, links, damping):
    count, comps, slices = sources.shape[:3]
    nev = eigvecs.shape[0]
    zdim = links.shape[3]
    devices = lax.axis_size(("src", "lat", "sub"))
    norm = math.sqrt(comps * slices * 128 * devices)
    f32 = jnp.float32

    src = sources.reshape(count * comps * slices, 128)
    eig = eigvecs.transpose(0, 2, 3, 1, 4).reshape(nev, slices, comps, 128)

    shape = lambda *dims: jax.ShapeDtypeStruct(dims, f32)
    lat, rest = lax.axis_size("lat"), lax.axis_size(("sub", "src"))
    hbm = lambda x: pltpu.with_memory_space_constraint(x, pltpu.HBM)
    slab = shape(4 * 18 * slices, 128)
    partial, eig, flat_links = call(
        functools.partial(correlation_kernel, nev=nev, slices=slices),
        (shape(lat, 8, 128), jax.ShapeDtypeStruct(eig.shape, eig.dtype), slab),
        4, 226_000_000, hbm=(0, 1, 2), smem=(3,),
        scratch=[
            pltpu.VMEM(src.shape, f32),
            pltpu.SemaphoreType.DMA((slices + 3,)),
        ],
    )(hbm(eig), hbm(src), hbm(links.reshape(4 * 18 * slices, zdim, 128)), damping)
    partial = lax.all_to_all(partial, "lat", 0, 0, tiled=True)
    partial = jnp.broadcast_to(partial.sum(0)[None], (rest, 8, 128))
    partial = lax.all_to_all(partial, ("sub", "src"), 0, 0, tiled=True)

    field = shape(slices, comps, 8, 128)
    z_halos = (shape(slices, 12, 8, 128),) * 2
    t_halos = (shape(12, 8, 128),) * 2
    flat = shape(count * comps * slices, 128)
    x, rate, guess, znear, zfar, tnear, tfar = call(
        functools.partial(guess_kernel, nev=nev, slices=slices, norm=norm),
        (field, shape(8, 128), pltpu.VMEM(flat.shape, f32)) + z_halos + t_halos,
        4, 226_000_000,
    )(partial, eigvals.reshape(1, nev), eig, flat_links)

    time = ("lat", "sub")

    def stage(kernel, outs, *args, scratch=(), hbm_outs=()):
        return call(
            functools.partial(kernel, slices=slices), outs, len(args),
            5_000_000, scratch=scratch, hbm_outs=hbm_outs,
        )(*args)

    carry = [pltpu.VMEM((12, 8, 128), f32)]
    zfar = swap(zfar, "src", True)
    znear = swap(znear, "src", False)
    tnear = swap(tnear, time, False)
    y = stage(local_kernel, field, x, src, flat_links, rate, scratch=carry)
    next_tnear, both_tfar = stage(
        edge_kernel, (shape(12, 8, 128), shape(2, 12, 8, 128)),
        y, flat_links, rate, znear, zfar, tfar,
    )
    both_tfar = swap(both_tfar, time, True)
    inner = slices - 2
    inner_x, inner_near, zinner = stage(
        inner_kernel,
        (shape(inner, comps, 8, 128), shape(inner, 12, 8, 128), shape(inner, 12, 8, 128)),
        y, flat_links, rate, znear, zfar,
    )
    zinner = swap(zinner, "src", True)
    next_tnear = swap(next_tnear, time, False)
    x, znear, zouter = stage(
        outer_kernel, (field, z_halos[0], shape(2, 12, 8, 128)),
        y, flat_links, rate, znear, zfar, tnear, both_tfar, inner_x, inner_near,
    )
    zouter = swap(zouter, "src", True)
    znear = swap(znear, "src", False)
    y, guess = stage(
        local_and_copy_kernel, (field, flat), x, src, flat_links, rate, guess,
        scratch=carry + [pltpu.SemaphoreType.DMA((8,))], hbm_outs=(1,),
    )
    x = stage(
        last_kernel, flat, y, flat_links, rate, znear, zinner, zouter, next_tnear, both_tfar,
        scratch=[pltpu.VMEM(flat.shape, f32), pltpu.SemaphoreType.DMA((8,))], hbm_outs=(0,),
    )
    return (guess.reshape(sources.shape), x.reshape(sources.shape))


def solution(mesh):
    return jax.shard_map(
        shards,
        mesh=mesh,
        in_specs=(
            P(None, None, ("lat", "sub"), "src", None),
            P(None, None, ("lat", "sub"), "src", None),
            P(),
            P(None, None, ("lat", "sub"), None, None),
            P("src"),
        ),
        out_specs=(
            P(None, None, ("lat", "sub"), "src", None),
            P(None, None, ("lat", "sub"), "src", None),
        ),
        check_vma=False,
    )
```
